32 devices in a mesh: dp: 16 (over z, x, core), seq: 2 (over y).
Axes of the slice: x: 2, y: 2, z: 4, core: 2. Of those that a mesh axis runs over, the one named last changes fastest.
Arguments:
- y_one: bfloat16 [16, 392, 576], P('dp', 'seq'), may hold values from -6 to 6
- second_stream: bfloat16 [16, 392, 576], P('dp', 'seq'), may hold values from -6 to 6
- d_one: bfloat16 [16, 392, 576], P('dp', 'seq'), may hold values from -6 to 6
- d_two: bfloat16 [16, 392, 576], P('dp', 'seq'), may hold values from -6 to 6
- layer_norm_gain: float32 [576], replicated, may hold values from 0.1 to 1.9
- w_qkv: bfloat16 [576, 1728], P('dp'), may hold values from -1 to 1
- w_out: bfloat16 [576, 576], P('dp'), may hold values from -0.25 to 0.25
- frames_valid: int32 [16], P('dp'), may hold values from 1 to 2, as said below
Outputs:
- x_one: bfloat16 [16, 392, 576], P('dp', 'seq')
- dx_two: bfloat16 [16, 392, 576], P('dp', 'seq')
- grad_qkv: float32 [576, 1728], P('dp', 'seq')
The draws below stay inside these ranges and needn't reach their ends.
Inputs may be any that keep to these rules, and one draw needn't show every extreme that they name: `frames_valid`: frames of a clip at or beyond its count are padding; some clip has all 2 frames and some clip has 1.
All inputs are finite; a program needn't handle non-finite values.
Results may differ from the reference program's by a relative error of at most 0.018.
The reference program's roundings to bfloat16 on the way count: a program that leaves them out, or rounds other values in their place, can miss the bound.
Values may be sent and summed in bfloat16 or wider, within the bound.
No kernel may reach another device: no remote copies, remote signals or barrier semaphores. Data moves between devices by JAX's collectives and lax.ppermute only.
A program may use at most 64 MiB of HBM per device.

```python
import math
import jax
import jax.numpy as jnp
from jax import lax

D = 576
HEADS = 8
HEAD = 72
SIDE = 14
POOL = 2
PSIDE = 7
FRAME_TOK = 196
PFRAME = 49
FRAMES = 2
TOK_DEV = 196
CLIPS = 16
N_SEQ = 2


def draw_frames_valid(key, part):
    first_key, second_key = jax.random.split(jax.random.fold_in(key, 7))
    counts = jax.random.randint(first_key, (CLIPS,), 1, FRAMES + 1, dtype=jnp.int32)
    order = jax.random.permutation(second_key, CLIPS)
    counts = counts.at[order[0]].set(FRAMES)
    counts = counts.at[order[1]].set(1)
    return counts.astype(jnp.int32)


def spiked(array, own_key, source, target, blocks, factor):
    def block_of(axis_at):
        return (jnp.arange(array.shape[axis_at]) // (array.shape[axis_at] // blocks)).reshape((-1,) + (1,) * (array.ndim - 1 - axis_at))

    near = jax.random.permutation(own_key, blocks)[block_of(target)]
    other_side = (block_of(target) + blocks // 2) % blocks
    return jnp.where((block_of(source) == near) | (block_of(source) == other_side), factor * array, array)


def levels(rng, dims, cuts, least, top_value):
    factor_of = 1.0
    for dim, shards_of in cuts:
        draws = jax.random.uniform(jax.random.fold_in(jax.random.fold_in(rng, 6), dim), (shards_of,), jnp.float32, least / len(cuts), top_value / len(cuts))
        factor_of = factor_of * jnp.repeat(jnp.exp(draws), dims[dim] // shards_of).reshape((-1,) + (1,) * (len(dims) - 1 - dim))
    return factor_of


def bell_draw(stream_key, dims, deviation, limit, pieces=(), kind=jnp.bfloat16):
    drawn = jax.random.normal(stream_key, dims, jnp.float32) * deviation
    if len(pieces) > 0:
        drawn = levels(stream_key, dims, pieces, -0.22, 0.18) * drawn
    return jnp.clip(drawn, min=-limit, max=limit).astype(kind)


def noise_with(stream_key, dims, deviation, bound, pieces, heavy, kind=jnp.bfloat16):
    result = deviation * jax.random.normal(stream_key, dims, jnp.float32)
    if pieces:
        result = result * levels(stream_key, dims, pieces, -0.22, 0.18)
    return jnp.clip(spiked(result, jax.random.fold_in(stream_key, 3), *heavy), -bound, bound).astype(kind)


def setup_inputs(seed: int = 0) -> dict:
    seeds = jax.random.split(jax.random.key(seed), 9)
    y_one = bell_draw(seeds[0], (CLIPS, FRAMES * FRAME_TOK, D), 1.0, 6.0, ((0, 16), (1, 2)))
    second_stream = noise_with(seeds[1], (CLIPS, FRAMES * FRAME_TOK, D), 1.0, 6.0, ((0, 16), (1, 2)), (0, 2, 16, 2.0))
    d_one = noise_with(seeds[2], (CLIPS, FRAMES * FRAME_TOK, D), 1.0, 6.0, ((0, 16), (1, 2)), (0, 2, 16, 2.0))
    d_two = bell_draw(seeds[3], (CLIPS, FRAMES * FRAME_TOK, D), 1.0, 6.0, ((0, 16), (1, 2)))
    layer_norm_gain = jnp.clip(1.0 + 0.18 * jax.random.normal(seeds[4], (D,), jnp.float32), 0.1, 1.9)
    w_qkv = bell_draw(seeds[5], (D, 3 * D), (D // 16) ** -0.5, 1.0, ((0, 16),))
    w_out = bell_draw(seeds[6], (D, D), D ** -0.5, 0.25, ((0, 16),))
    frames_valid = draw_frames_valid(jax.random.fold_in(seeds[8], 71), 0)
    return dict(y_one=y_one, second_stream=second_stream, d_one=d_one, d_two=d_two, layer_norm_gain=layer_norm_gain, w_qkv=w_qkv, w_out=w_out, frames_valid=frames_valid)


def pool_table():
    token_ids = jnp.arange(FRAME_TOK, dtype=jnp.int32)
    pooled_ids = jnp.arange(PFRAME, dtype=jnp.int32)
    token_row = token_ids // SIDE // POOL
    token_col = token_ids % SIDE // POOL
    hits = ((token_row[None, :] == (pooled_ids // PSIDE)[:, None]) & (token_col[None, :] == (pooled_ids % PSIDE)[:, None])).astype(jnp.float32)
    return hits / lax.optimization_barrier(jnp.sum(hits, axis=1, keepdims=True))

def normalize_rows(inputs):
    values = inputs.astype(jnp.float32)
    centered = values - lax.optimization_barrier(jnp.mean(values, axis=-1, keepdims=True))
    inverse_deviation = lax.rsqrt(lax.optimization_barrier(jnp.mean(centered * centered, axis=-1, keepdims=True)) + 1e-05)
    return (centered * inverse_deviation, inverse_deviation)

def pool_rows(table, rows):
    frame_count = rows.shape[0] // FRAME_TOK
    shaped = rows.reshape(frame_count, FRAME_TOK, rows.shape[1])
    pooled = jnp.einsum('pt,ftw->fpw', table, shaped, precision=lax.Precision.HIGHEST)
    return pooled.reshape(frame_count * PFRAME, rows.shape[1])

def spread_rows(table, pooled):
    frame_count = pooled.shape[0] // PFRAME
    shaped = pooled.reshape(frame_count, PFRAME, pooled.shape[1])
    spread = jnp.einsum('pt,fpw->ftw', table, shaped, precision=lax.Precision.HIGHEST)
    return spread.reshape(frame_count * FRAME_TOK, pooled.shape[1])

def round_parts(parts):
    rounded = lax.optimization_barrier(parts.astype(jnp.bfloat16))
    return lax.optimization_barrier(jnp.sum(rounded.astype(jnp.float32), axis=0))

def masked_softmax(scores, key_live):
    masked = jnp.where(key_live[None, None, :], scores, -jnp.inf)
    top = lax.optimization_barrier(jnp.max(masked, axis=-1, keepdims=True))
    raised = jnp.exp(masked - top)
    return raised / lax.optimization_barrier(jnp.sum(raised, axis=-1, keepdims=True))

def reference(y_one, second_stream, d_one, d_two, layer_norm_gain, w_qkv, w_out, frames_valid):
    table = pool_table()
    scale = 1.0 / math.sqrt(HEAD)
    grad_scale = 1.0 / math.sqrt(CLIPS * FRAMES * FRAME_TOK)
    tokens_clip = FRAMES * FRAME_TOK
    keys_clip = FRAMES * PFRAME

    def clip_step(carry, inputs):
        upper, lower_stream, cot_one, cot_two, count = inputs
        standardized_input, inverse_deviation = normalize_rows(lower_stream)
        normed_rows = (standardized_input * layer_norm_gain).astype(jnp.bfloat16)
        projected = jnp.dot(normed_rows, w_qkv, preferred_element_type=jnp.float32)
        queries = projected[:, :D].astype(jnp.bfloat16)
        pooled = pool_rows(table, projected[:, D:]).astype(jnp.bfloat16)
        key_live = jnp.arange(keys_clip, dtype=jnp.int32) // PFRAME < count
        query_heads = queries.astype(jnp.float32).reshape(tokens_clip, HEADS, HEAD)
        key_heads = pooled[:, :D].astype(jnp.float32).reshape(keys_clip, HEADS, HEAD)
        value_heads = pooled[:, D:].astype(jnp.float32).reshape(keys_clip, HEADS, HEAD)
        scores = jnp.einsum('nhe,mhe->hnm', query_heads, key_heads) * scale
        probs = masked_softmax(scores, key_live).astype(jnp.bfloat16)
        probs_wide = probs.astype(jnp.float32)
        mixed_wide = jnp.einsum('hnm,mhe->nhe', probs_wide, value_heads)
        mixed = mixed_wide.reshape(tokens_clip, D).astype(jnp.bfloat16)
        branch = jnp.dot(mixed, w_out, preferred_element_type=jnp.float32)
        x_one = (upper.astype(jnp.float32) - branch).astype(jnp.bfloat16)
        d_mixed = jnp.dot(cot_one, w_out.T, preferred_element_type=jnp.float32).astype(jnp.bfloat16)
        d_heads = d_mixed.astype(jnp.float32).reshape(tokens_clip, HEADS, HEAD)
        d_probs = jnp.einsum('nhe,mhe->hnm', d_heads, value_heads)
        delta = jnp.einsum('nhe,nhe->hn', d_heads, mixed_wide)
        d_scores = (probs_wide * (d_probs - delta[:, :, None]) * scale).astype(jnp.bfloat16)
        d_scores_wide = d_scores.astype(jnp.float32)
        d_queries = jnp.einsum('hnm,mhe->nhe', d_scores_wide, key_heads).reshape(tokens_clip, D).astype(jnp.bfloat16)
        split_scores = d_scores_wide.reshape(HEADS, N_SEQ, TOK_DEV, keys_clip)
        split_probs = probs_wide.reshape(HEADS, N_SEQ, TOK_DEV, keys_clip)
        split_queries = query_heads.reshape(N_SEQ, TOK_DEV, HEADS, HEAD)
        split_grads = d_heads.reshape(N_SEQ, TOK_DEV, HEADS, HEAD)
        key_parts = jnp.einsum('hsnm,snhe->smhe', split_scores, split_queries).reshape(N_SEQ, keys_clip, D)
        value_parts = jnp.einsum('hsnm,snhe->smhe', split_probs, split_grads).reshape(N_SEQ, keys_clip, D)
        d_pooled = jnp.concatenate([round_parts(key_parts), round_parts(value_parts)], axis=1)
        d_tokens = spread_rows(table, d_pooled).astype(jnp.bfloat16)
        d_projected = jnp.concatenate([d_queries, d_tokens], axis=1)
        d_normed = jnp.dot(d_projected, w_qkv.T, preferred_element_type=jnp.float32)
        gain_applied = d_normed * layer_norm_gain
        lower_gradient = inverse_deviation * (gain_applied - lax.optimization_barrier(jnp.mean(gain_applied, axis=-1, keepdims=True)) - standardized_input * lax.optimization_barrier(jnp.mean(gain_applied * standardized_input, axis=-1, keepdims=True)))
        dx_two = (cot_two.astype(jnp.float32) + lower_gradient).astype(jnp.bfloat16)
        qkv_parts = jnp.einsum('snd,snk->sdk', normed_rows.astype(jnp.float32).reshape(N_SEQ, TOK_DEV, D), d_projected.astype(jnp.float32).reshape(N_SEQ, TOK_DEV, 3 * D)) * grad_scale
        new_carry = carry + round_parts(qkv_parts)
        return (new_carry, (x_one, dx_two))
    start = jnp.zeros((D, 3 * D), jnp.float32)
    total, streams = lax.scan(clip_step, start, (y_one, second_stream, d_one, d_two, frames_valid))
    return (streams[0], streams[1], total)
```

```python
import functools
import math

import jax
import jax.numpy as jnp
from jax import lax
from jax.experimental import pallas as pl
from jax.experimental.pallas import tpu as pltpu
from jax.sharding import PartitionSpec as P

HEADS = 8
SIDE = 14
POOL = 2
PSIDE = 7
FRAME_TOK = 196
PFRAME = 49


def pool_table():
    token_ids = jnp.arange(FRAME_TOK, dtype=jnp.int32)
    pooled_ids = jnp.arange(PFRAME, dtype=jnp.int32)
    token_row = token_ids // SIDE // POOL
    token_col = token_ids % SIDE // POOL
    hits = (
        (token_row[None, :] == (pooled_ids // PSIDE)[:, None])
        & (token_col[None, :] == (pooled_ids % PSIDE)[:, None])
    ).astype(jnp.float32)
    return hits / jnp.sum(hits, axis=1, keepdims=True)


def normalize_rows(inputs):
    values = inputs.astype(jnp.float32)
    centered = values - jnp.mean(values, axis=-1, keepdims=True)
    inverse_deviation = lax.rsqrt(jnp.mean(centered * centered, axis=-1, keepdims=True) + 1e-05)
    return (centered * inverse_deviation, inverse_deviation)


def pool_rows(table, rows):
    frame_count = rows.shape[0] // FRAME_TOK
    shaped = rows.reshape(frame_count, FRAME_TOK, rows.shape[1])
    pooled = jnp.einsum("pt,ftw->fpw", table, shaped, precision=lax.Precision.HIGHEST)
    return pooled.reshape(frame_count * PFRAME, rows.shape[1])


def spread_rows(table, pooled):
    frame_count = pooled.shape[0] // PFRAME
    shaped = pooled.reshape(frame_count, PFRAME, pooled.shape[1])
    spread = jnp.einsum("pt,fpw->ftw", table, shaped, precision=lax.Precision.HIGHEST)
    return spread.reshape(frame_count * FRAME_TOK, pooled.shape[1])


def masked_softmax(scores, key_live):
    masked = jnp.where(key_live[None, None, :], scores, -jnp.inf)
    top = jnp.max(masked, axis=-1, keepdims=True)
    raised = jnp.exp(masked - top)
    return raised / jnp.sum(raised, axis=-1, keepdims=True)


def local_general(y_one, second_stream, d_one, d_two, layer_norm_gain, w_qkv, w_out, frames_valid):
    seq_count = lax.axis_size("seq")
    clip_count = lax.axis_size("dp")
    model_width = w_out.shape[1]
    tokens_here = second_stream.shape[1]
    head_width = model_width // HEADS
    full_qkv, full_out = (
        lax.all_gather(w_qkv, "dp", axis=0, tiled=True),
        lax.all_gather(w_out, "dp", axis=0, tiled=True),
    )
    table = pool_table()
    scale = 1.0 / math.sqrt(head_width)
    grad_scale = 1.0 / math.sqrt(clip_count * seq_count * tokens_here)
    upper = y_one[0]
    cot_one = d_one[0]
    standardized_input, inverse_deviation = normalize_rows(second_stream[0])
    normed_rows = (standardized_input * layer_norm_gain).astype(jnp.bfloat16)
    projected = jnp.dot(normed_rows, full_qkv, preferred_element_type=jnp.float32)
    queries = projected[:, :model_width].astype(jnp.bfloat16)
    own_pooled = pool_rows(table, projected[:, model_width:]).astype(jnp.bfloat16)
    all_pooled = lax.all_gather(own_pooled, "seq", axis=0, tiled=True)
    key_total = all_pooled.shape[0]
    key_live = jnp.arange(key_total, dtype=jnp.int32) // PFRAME < frames_valid[0]
    query_heads = queries.reshape(tokens_here, HEADS, head_width)
    key_heads = all_pooled[:, :model_width].reshape(key_total, HEADS, head_width)
    value_heads = all_pooled[:, model_width:].reshape(key_total, HEADS, head_width)
    scores = (
        jnp.einsum("nhe,mhe->hnm", query_heads, key_heads, preferred_element_type=jnp.float32)
        * scale
    )
    probs = masked_softmax(scores, key_live).astype(jnp.bfloat16)
    mixed_wide = jnp.einsum("hnm,mhe->nhe", probs, value_heads, preferred_element_type=jnp.float32)
    mixed = mixed_wide.reshape(tokens_here, model_width).astype(jnp.bfloat16)
    branch = jnp.dot(mixed, full_out, preferred_element_type=jnp.float32)
    x_one = (upper.astype(jnp.float32) - branch).astype(jnp.bfloat16)
    d_mixed = lax.dot_general(
        cot_one, full_out, (((1,), (1,)), ((), ())), preferred_element_type=jnp.float32
    ).astype(jnp.bfloat16)
    d_heads = d_mixed.reshape(tokens_here, HEADS, head_width)
    d_probs = jnp.einsum("nhe,mhe->hnm", d_heads, value_heads, preferred_element_type=jnp.float32)
    delta = jnp.einsum("nhe,nhe->hn", d_heads.astype(jnp.float32), mixed_wide)
    d_scores = (probs.astype(jnp.float32) * (d_probs - delta[:, :, None]) * scale).astype(
        jnp.bfloat16
    )
    d_queries = (
        jnp.einsum("hnm,mhe->nhe", d_scores, key_heads, preferred_element_type=jnp.float32)
        .reshape(tokens_here, model_width)
        .astype(jnp.bfloat16)
    )
    key_term = jnp.einsum(
        "hnm,nhe->mhe", d_scores, query_heads, preferred_element_type=jnp.float32
    ).reshape(key_total, model_width)
    value_term = jnp.einsum(
        "hnm,nhe->mhe", probs, d_heads, preferred_element_type=jnp.float32
    ).reshape(key_total, model_width)
    own_grads = lax.psum_scatter(
        jnp.concatenate([key_term, value_term], axis=1).astype(jnp.bfloat16),
        "seq",
        scatter_dimension=0,
        tiled=True,
    ).astype(jnp.float32)
    d_tokens = spread_rows(table, own_grads).astype(jnp.bfloat16)
    d_projected = jnp.concatenate([d_queries, d_tokens], axis=1)
    d_normed = lax.dot_general(
        d_projected, full_qkv, (((1,), (1,)), ((), ())), preferred_element_type=jnp.float32
    )
    gain_applied = d_normed * layer_norm_gain
    lower_gradient = inverse_deviation * (
        gain_applied
        - jnp.mean(gain_applied, axis=-1, keepdims=True)
        - standardized_input * jnp.mean(gain_applied * standardized_input, axis=-1, keepdims=True)
    )
    dx_two = (d_two[0].astype(jnp.float32) + lower_gradient).astype(jnp.bfloat16)
    qkv_term = (
        lax.dot_general(
            normed_rows, d_projected, (((0,), (0,)), ((), ())), preferred_element_type=jnp.float32
        )
        * grad_scale
    )
    column_qkv = lax.psum_scatter(
        qkv_term.astype(jnp.bfloat16), "seq", scatter_dimension=1, tiled=True
    ).astype(jnp.float32)
    grad_qkv = lax.psum_scatter(column_qkv, "dp", scatter_dimension=0, tiled=True)
    return (x_one[None], dx_two[None], grad_qkv)


AXES = ("dp", "seq")
OVER_Y, OVER_CORE, OVER_X, OVER_Z1, OVER_Z2 = 1, 2, 4, 8, 16

D = 576
HALF = 288
HEAD = 72
HERE = 4
ROWS = 36
SLOT = 48
REL = 16 * SLOT
FSLOT = 208
TOK2 = 2 * FSLOT
KEYS = 128
KLANES = HERE * KEYS
QKV = 3 * HALF
SHARD = QKV + D
SEND = 640 + HALF
BF16, F32 = jnp.bfloat16, jnp.float32


def swap(array, mask):
    return lax.ppermute(array, AXES, [(i, i ^ mask) for i in range(32)])


def dot(a, b, dims=((1,), (0,))):
    return lax.dot_general(a, b, (dims, ((), ())), preferred_element_type=F32)


NT = ((1,), (1,))
TN = ((0,), (0,))


def iota(shape, dim):
    return lax.broadcasted_iota(jnp.int32, shape, dim)


def feature_of_slot(shape, dim):
    me = lax.axis_index("dp")
    at = iota(shape, dim)
    feature = jnp.full(shape, -1, jnp.int32)
    for s in range(16):
        rel = ((s & 7) << 1) | (s >> 3)
        here = (at >= SLOT * s) & (at < SLOT * s + ROWS)
        feature = jnp.where(here, (me ^ rel) * ROWS + at - SLOT * s, feature)
    return feature


def one_hot(hits):
    return jnp.where(hits, 1.0, 0.0).astype(BF16)


def key_of_token(shape, dim):
    at = iota(shape, dim)
    second = at >= FSLOT
    t = jnp.where(second, at - FSLOT, at)
    row = (t * 9363) >> 17
    col = t - row * SIDE
    key = (row >> 1) * PSIDE + (col >> 1) + jnp.where(second, 64, 0)
    return jnp.where(t < FRAME_TOK, key, -1)


def shard_kernel(qkv_ref, out_ref, own_ref):
    y = lax.axis_index("seq")
    for s in range(2):

        @pl.when(y == s)
        def _():
            for part in range(3):
                at = part * D + s * HALF
                own_ref[:, part * HALF : (part + 1) * HALF] = qkv_ref[:, at : at + HALF]

    own_ref[:, QKV:] = out_ref[...]


def standardize(values):
    centered = values - jnp.mean(values, axis=-1, keepdims=True)
    inverse = lax.rsqrt(jnp.mean(centered * centered, axis=-1, keepdims=True) + 1e-05)
    return centered * inverse, inverse


def prep_kernel(own_ref, peer_ref, gain_ref, rel_ref, relt_ref, pool_ref, poolt_ref):
    order = one_hot(iota((D, REL), 0) == feature_of_slot((1, REL), 1))
    order_t = one_hot(feature_of_slot((REL, 1), 0) == iota((REL, D), 1))
    gain = gain_ref[...]
    for f, src in enumerate((own_ref, peer_ref)):
        normed = (standardize(src[...].astype(F32))[0] * gain).astype(BF16)
        normed = jnp.concatenate([normed, jnp.zeros((FSLOT - FRAME_TOK, D), BF16)], axis=0)
        rel_ref[f * FSLOT : (f + 1) * FSLOT, :] = dot(normed, order).astype(BF16)
        relt_ref[f] = dot(order_t, normed, NT).astype(BF16)
    table = one_hot(iota((KEYS, TOK2), 0) == key_of_token((1, TOK2), 1)) * BF16(0.25)
    pooled = dot(table, rel_ref[...])
    hi = pooled.astype(BF16)
    pool_ref[:KEYS, :] = hi
    pool_ref[KEYS:, :] = (pooled - hi.astype(F32)).astype(BF16)
    pooled_t = dot(relt_ref[0], table[:, :FSLOT], NT) + dot(relt_ref[1], table[:, FSLOT:], NT)
    hi_t = pooled_t.astype(BF16)
    poolt_ref[:, :KEYS] = hi_t
    poolt_ref[:, KEYS:] = (pooled_t - hi_t.astype(F32)).astype(BF16)


def head_lanes(h):
    lane = iota((1, HALF), 1)
    return (lane >= h * HEAD) & (lane < (h + 1) * HEAD)


def main_kernel(grad_scale, valid_ref, rel_ref, relt_ref, pool_ref, poolt_ref, down_ref, dpeer_ref, *rest):
    blocks = rest[:16]
    gown_ref, goth_ref, w_ref, dq_ref, e_ref, mixed_ref, outh_ref = rest[16:23]
    cot_ref, kbig_ref, vbig_ref, s_ref, p_ref, ds_ref, g_ref = rest[23:]
    y = lax.axis_index("seq")
    scale = 1.0 / math.sqrt(HEAD)
    for s in range(16):
        w_ref[s * SLOT + 32 : (s + 1) * SLOT, :] = jnp.zeros((16, SHARD), BF16)
        w_ref[s * SLOT : s * SLOT + ROWS, :] = blocks[s][...]
    for f, src in enumerate((down_ref, dpeer_ref)):
        at = f * FSLOT
        cot_ref[at + 192 : at + FSLOT, :] = jnp.zeros((16, D), BF16)
        cot_ref[at : at + FRAME_TOK, :] = src[...]

    queries = dot(rel_ref[...], w_ref[:, :HALF]).astype(BF16)
    kv = dot(pool_ref[...], w_ref[:, 256:QKV])
    kv = kv[:KEYS] + kv[KEYS:]
    keys = kv[:, 32 : 32 + HALF].astype(BF16)
    values = kv[:, 32 + HALF :].astype(BF16)
    for h in range(HERE):
        lanes = head_lanes(h)
        kbig_ref[h * KEYS : (h + 1) * KEYS, :] = jnp.where(lanes, keys, BF16(0))
        vbig_ref[h * KEYS : (h + 1) * KEYS, :] = jnp.where(lanes, values, BF16(0))
    select = one_hot(iota((HALF, REL), 0) + HALF * y == feature_of_slot((1, REL), 1))
    outh_ref[...] = dot(select, w_ref[:, QKV:]).astype(BF16)
    d_mixed = dot(cot_ref[...], outh_ref[...], NT).astype(BF16)

    s_ref[...] = dot(queries, kbig_ref[...], NT)
    key = iota((1, KEYS), 1)
    late = key >= 64
    frame = jnp.where(late, 1 - y, y)
    live = (jnp.where(late, key - 64, key) < PFRAME) & (frame < valid_ref[0])
    for h in range(HERE):
        cols = slice(h * KEYS, (h + 1) * KEYS)
        for f in range(2):
            rows = slice(f * FSLOT, (f + 1) * FSLOT)
            masked = jnp.where(live, s_ref[rows, cols] * scale, -jnp.inf)
            raised = jnp.exp(masked - jnp.max(masked, axis=-1, keepdims=True))
            p_ref[rows, cols] = (raised / jnp.sum(raised, axis=-1, keepdims=True)).astype(BF16)
    mixed_ref[...] = dot(p_ref[...], vbig_ref[...]).astype(BF16)
    s_ref[...] = dot(d_mixed, vbig_ref[...], NT)
    for h in range(HERE):
        cols = slice(h * KEYS, (h + 1) * KEYS)
        for f in range(2):
            rows = slice(f * FSLOT, (f + 1) * FSLOT)
            wide = p_ref[rows, cols].astype(F32)
            d_probs = s_ref[rows, cols]
            delta = jnp.sum(wide * d_probs, axis=-1, keepdims=True)
            ds_ref[rows, cols] = (wide * (d_probs - delta) * scale).astype(BF16)
    dq_ref[:, 256:384] = jnp.zeros((TOK2, 128), BF16)
    dq_ref[:, :HALF] = dot(ds_ref[...], kbig_ref[...]).astype(BF16)

    def by_head(big):
        return sum(jnp.where(head_lanes(h), big[h * KEYS : (h + 1) * KEYS], 0.0) for h in range(HERE))

    d_keys = by_head(dot(ds_ref[...], queries, TN)) * 0.25
    d_values = by_head(dot(p_ref[...], d_mixed, TN)) * 0.25
    e = jnp.concatenate([jnp.zeros((KEYS, 32), F32), d_keys, d_values], axis=1).astype(BF16)
    e_ref[:KEYS, :] = e
    e_ref[KEYS:, :] = e
    dq = dq_ref[...]
    g_q = dot(relt_ref[0], dq[:FSLOT]) + dot(relt_ref[1], dq[FSLOT:])
    g_kv = dot(poolt_ref[...], e_ref[...]) * 4.0
    g_ref[:, :256] = g_q[:, :256] * grad_scale
    g_ref[:, 256:384] = (g_q[:, 256:] + g_kv[:, :128]) * grad_scale
    g_ref[:, 384:] = g_kv[:, 128:] * grad_scale
    for s in range(8):
        gown_ref[s] = g_ref[s * SLOT : s * SLOT + ROWS, :].astype(BF16)
        goth_ref[s] = g_ref[(s + 8) * SLOT : (s + 8) * SLOT + ROWS, :].astype(BF16)


def cross_kernel(w_ref, dq_ref, e_ref, mixed_ref, send_ref, dn_ref, oth_ref):
    y = lax.axis_index("seq")
    feature = feature_of_slot((1, REL), 1)
    order = one_hot(iota((D, REL), 0) == feature)
    natural = dot(order, w_ref[:, :QKV]).astype(BF16)
    spread = one_hot(key_of_token((TOK2, 1), 0) == iota((TOK2, KEYS), 1))
    d_tokens = dot(spread, e_ref[:KEYS, :]).astype(BF16)
    d_normed = dot(dq_ref[...], natural[:, :384], NT) + dot(d_tokens, natural[:, 256:], NT)
    dn_ref[...] = d_normed[:FRAME_TOK]
    send_ref[:, :D] = d_normed[FSLOT : FSLOT + FRAME_TOK].astype(BF16)
    send_ref[:, D:640] = jnp.zeros((FRAME_TOK, 640 - D), BF16)
    send_ref[:, 640:] = mixed_ref[FSLOT : FSLOT + FRAME_TOK, :]
    select = one_hot(iota((HALF, REL), 0) + HALF * (1 - y) == feature)
    oth_ref[...] = dot(select, w_ref[:, QKV:]).astype(BF16)


def last_kernel(yone_ref, second_ref, dtwo_ref, gain_ref, got_ref, dn_ref, mixed_ref, outh_ref, oth_ref, x_ref, dx_ref):
    branch = dot(mixed_ref[:FRAME_TOK, :], outh_ref[...]) + dot(got_ref[:, 640:], oth_ref[...])
    x_ref[...] = (yone_ref[...].astype(F32) - branch).astype(BF16)
    xhat, inverse = standardize(second_ref[...].astype(F32))
    gained = (dn_ref[...] + got_ref[:, :D].astype(F32)) * gain_ref[...]
    lower = inverse * (
        gained
        - jnp.mean(gained, axis=-1, keepdims=True)
        - xhat * jnp.mean(gained * xhat, axis=-1, keepdims=True)
    )
    dx_ref[...] = (dtwo_ref[...].astype(F32) + lower).astype(BF16)


def shape(*dims, kind=BF16):
    return jax.ShapeDtypeStruct(dims, kind)


def call(kernel, outs, args, scratch=(), smem=0, flops=0, moved=0, name=None, limit=16):
    vmem = pl.BlockSpec(memory_space=pltpu.VMEM)
    return pl.pallas_call(
        kernel,
        out_shape=outs,
        in_specs=[pl.BlockSpec(memory_space=pltpu.SMEM)] * smem + [vmem] * (len(args) - smem),
        out_specs=jax.tree.map(lambda _: vmem, outs),
        scratch_shapes=scratch,
        compiler_params=pltpu.CompilerParams(vmem_limit_bytes=limit << 20),
        cost_estimate=pl.CostEstimate(flops=flops, bytes_accessed=moved, transcendentals=0),
        name=name,
    )(*args)


def local_paired(y_one, second_stream, d_one, d_two, layer_norm_gain, w_qkv, w_out, frames_valid):
    grad_scale = 1.0 / math.sqrt(lax.axis_size("dp") * 2 * FRAME_TOK)
    y = lax.axis_index("seq")
    second, cot = second_stream[0], d_one[0]
    gain = layer_norm_gain.reshape(1, D)

    own = call(shard_kernel, shape(ROWS, SHARD), (w_qkv, w_out), moved=400_000, name="shard")
    by_b = swap(own, OVER_Z2)
    by_x = swap(own, OVER_X)
    by_a = swap(own, OVER_Z1)
    second_peer = swap(second, OVER_Y)
    cot_peer = swap(cot, OVER_Y)
    by_ab = swap(by_b, OVER_Z1)
    by_xb = swap(by_b, OVER_X)
    by_xa = swap(by_a, OVER_X)
    by_xab = swap(by_ab, OVER_X)
    mine = (own, by_x, by_a, by_xa, by_b, by_xb, by_ab, by_xab)
    other = tuple(swap(block, OVER_CORE) for block in mine)

    rel, rel_t, pool, pool_t = call(
        prep_kernel,
        (shape(TOK2, REL), shape(2, REL, FSLOT), shape(2 * KEYS, REL), shape(REL, 2 * KEYS)),
        (second, second_peer, gain),
        flops=1_200_000_000,
        moved=3_000_000,
        name="prep",
    )
    g_own, g_oth, w_rel, d_q, e, mixed, out_own = call(
        functools.partial(main_kernel, grad_scale),
        (
            shape(8, ROWS, QKV),
            shape(8, ROWS, QKV),
            shape(REL, SHARD),
            shape(TOK2, 384),
            shape(2 * KEYS, 608),
            shape(TOK2, HALF),
            shape(HALF, D),
        ),
        (frames_valid, rel, rel_t, pool, pool_t, cot, cot_peer) + mine + other,
        scratch=(
            pltpu.VMEM((TOK2, D), BF16),
            pltpu.VMEM((KLANES, HALF), BF16),
            pltpu.VMEM((KLANES, HALF), BF16),
            pltpu.VMEM((TOK2, KLANES), F32),
            pltpu.VMEM((TOK2, KLANES), BF16),
            pltpu.VMEM((TOK2, KLANES), BF16),
            pltpu.VMEM((REL, QKV), F32),
        ),
        smem=1,
        flops=4_000_000_000,
        moved=8_000_000,
        name="main",
        limit=32,
    )

    def add(a, b):
        return (a.astype(F32) + b.astype(F32)).astype(BF16)

    chunk = add(g_own, swap(g_oth, OVER_CORE))
    r_ab, r_b, r_a, r_s = (swap(chunk[i], OVER_X) for i in (7, 5, 3, 1))
    q_b = swap(add(chunk[6], r_ab), OVER_Z1)
    q_s = swap(add(chunk[2], r_a), OVER_Z1)
    last = swap(add(add(chunk[4], r_b), q_b), OVER_Z2)
    total = chunk[0].astype(F32) + r_s.astype(F32) + q_s.astype(F32) + last.astype(F32)
    g_q, g_k, g_v = total[:, :HALF], total[:, HALF : 2 * HALF], total[:, 2 * HALF :]
    first = y == 0
    crossed = swap(jnp.where(first, g_v, g_q), OVER_Y)
    grad_qkv = jnp.concatenate([jnp.where(first, g_q, g_k), crossed, jnp.where(first, g_k, g_v)], axis=1)

    send, d_normed, out_oth = call(
        cross_kernel,
        (shape(FRAME_TOK, SEND), shape(FRAME_TOK, D, kind=F32), shape(HALF, D)),
        (w_rel, d_q, e, mixed),
        flops=2_000_000_000,
        moved=4_000_000,
        name="cross",
    )
    got = swap(send, OVER_Y)
    x_one, dx_two = call(
        last_kernel,
        (shape(FRAME_TOK, D), shape(FRAME_TOK, D)),
        (y_one[0], second, d_two[0], gain, got, d_normed, mixed, out_own, out_oth),
        flops=300_000_000,
        moved=3_000_000,
        name="last",
    )
    return (x_one[None], dx_two[None], grad_qkv)


def solution(mesh):
    in_specs = (
        P("dp", "seq", None),
        P("dp", "seq", None),
        P("dp", "seq", None),
        P("dp", "seq", None),
        P(),
        P("dp", None),
        P("dp", None),
        P("dp"),
    )
    out_specs = (P("dp", "seq", None), P("dp", "seq", None), P("dp", "seq"))
    local = local_paired if dict(mesh.shape) == {"dp": 16, "seq": 2} else local_general
    return jax.shard_map(local, mesh=mesh, in_specs=in_specs, out_specs=out_specs, check_vma=False)
```

```python
import functools
import math

import jax
import jax.numpy as jnp
from jax import lax
from jax.experimental import pallas as pl
from jax.experimental.pallas import tpu as pltpu
from jax.sharding import PartitionSpec as P

HEADS = 8
SIDE = 14
POOL = 2
PSIDE = 7
FRAME_TOK = 196
PFRAME = 49


def pool_table():
    token_ids = jnp.arange(FRAME_TOK, dtype=jnp.int32)
    pooled_ids = jnp.arange(PFRAME, dtype=jnp.int32)
    token_row = token_ids // SIDE // POOL
    token_col = token_ids % SIDE // POOL
    hits = (
        (token_row[None, :] == (pooled_ids // PSIDE)[:, None])
        & (token_col[None, :] == (pooled_ids % PSIDE)[:, None])
    ).astype(jnp.float32)
    return hits / jnp.sum(hits, axis=1, keepdims=True)


def normalize_rows(inputs):
    values = inputs.astype(jnp.float32)
    centered = values - jnp.mean(values, axis=-1, keepdims=True)
    inverse_deviation = lax.rsqrt(jnp.mean(centered * centered, axis=-1, keepdims=True) + 1e-05)
    return (centered * inverse_deviation, inverse_deviation)


def pool_rows(table, rows):
    frame_count = rows.shape[0] // FRAME_TOK
    shaped = rows.reshape(frame_count, FRAME_TOK, rows.shape[1])
    pooled = jnp.einsum("pt,ftw->fpw", table, shaped, precision=lax.Precision.HIGHEST)
    return pooled.reshape(frame_count * PFRAME, rows.shape[1])


def spread_rows(table, pooled):
    frame_count = pooled.shape[0] // PFRAME
    shaped = pooled.reshape(frame_count, PFRAME, pooled.shape[1])
    spread = jnp.einsum("pt,fpw->ftw", table, shaped, precision=lax.Precision.HIGHEST)
    return spread.reshape(frame_count * FRAME_TOK, pooled.shape[1])


def masked_softmax(scores, key_live):
    masked = jnp.where(key_live[None, None, :], scores, -jnp.inf)
    top = jnp.max(masked, axis=-1, keepdims=True)
    raised = jnp.exp(masked - top)
    return raised / jnp.sum(raised, axis=-1, keepdims=True)


def local_general(y_one, second_stream, d_one, d_two, layer_norm_gain, w_qkv, w_out, frames_valid):
    seq_count = lax.axis_size("seq")
    clip_count = lax.axis_size("dp")
    model_width = w_out.shape[1]
    tokens_here = second_stream.shape[1]
    head_width = model_width // HEADS
    full_qkv, full_out = (
        lax.all_gather(w_qkv, "dp", axis=0, tiled=True),
        lax.all_gather(w_out, "dp", axis=0, tiled=True),
    )
    table = pool_table()
    scale = 1.0 / math.sqrt(head_width)
    grad_scale = 1.0 / math.sqrt(clip_count * seq_count * tokens_here)
    upper = y_one[0]
    cot_one = d_one[0]
    standardized_input, inverse_deviation = normalize_rows(second_stream[0])
    normed_rows = (standardized_input * layer_norm_gain).astype(jnp.bfloat16)
    projected = jnp.dot(normed_rows, full_qkv, preferred_element_type=jnp.float32)
    queries = projected[:, :model_width].astype(jnp.bfloat16)
    own_pooled = pool_rows(table, projected[:, model_width:]).astype(jnp.bfloat16)
    all_pooled = lax.all_gather(own_pooled, "seq", axis=0, tiled=True)
    key_total = all_pooled.shape[0]
    key_live = jnp.arange(key_total, dtype=jnp.int32) // PFRAME < frames_valid[0]
    query_heads = queries.reshape(tokens_here, HEADS, head_width)
    key_heads = all_pooled[:, :model_width].reshape(key_total, HEADS, head_width)
    value_heads = all_pooled[:, model_width:].reshape(key_total, HEADS, head_width)
    scores = (
        jnp.einsum("nhe,mhe->hnm", query_heads, key_heads, preferred_element_type=jnp.float32)
        * scale
    )
    probs = masked_softmax(scores, key_live).astype(jnp.bfloat16)
    mixed_wide = jnp.einsum("hnm,mhe->nhe", probs, value_heads, preferred_element_type=jnp.float32)
    mixed = mixed_wide.reshape(tokens_here, model_width).astype(jnp.bfloat16)
    branch = jnp.dot(mixed, full_out, preferred_element_type=jnp.float32)
    x_one = (upper.astype(jnp.float32) - branch).astype(jnp.bfloat16)
    d_mixed = lax.dot_general(
        cot_one, full_out, (((1,), (1,)), ((), ())), preferred_element_type=jnp.float32
    ).astype(jnp.bfloat16)
    d_heads = d_mixed.reshape(tokens_here, HEADS, head_width)
    d_probs = jnp.einsum("nhe,mhe->hnm", d_heads, value_heads, preferred_element_type=jnp.float32)
    delta = jnp.einsum("nhe,nhe->hn", d_heads.astype(jnp.float32), mixed_wide)
    d_scores = (probs.astype(jnp.float32) * (d_probs - delta[:, :, None]) * scale).astype(
        jnp.bfloat16
    )
    d_queries = (
        jnp.einsum("hnm,mhe->nhe", d_scores, key_heads, preferred_element_type=jnp.float32)
        .reshape(tokens_here, model_width)
        .astype(jnp.bfloat16)
    )
    key_term = jnp.einsum(
        "hnm,nhe->mhe", d_scores, query_heads, preferred_element_type=jnp.float32
    ).reshape(key_total, model_width)
    value_term = jnp.einsum(
        "hnm,nhe->mhe", probs, d_heads, preferred_element_type=jnp.float32
    ).reshape(key_total, model_width)
    own_grads = lax.psum_scatter(
        jnp.concatenate([key_term, value_term], axis=1).astype(jnp.bfloat16),
        "seq",
        scatter_dimension=0,
        tiled=True,
    ).astype(jnp.float32)
    d_tokens = spread_rows(table, own_grads).astype(jnp.bfloat16)
    d_projected = jnp.concatenate([d_queries, d_tokens], axis=1)
    d_normed = lax.dot_general(
        d_projected, full_qkv, (((1,), (1,)), ((), ())), preferred_element_type=jnp.float32
    )
    gain_applied = d_normed * layer_norm_gain
    lower_gradient = inverse_deviation * (
        gain_applied
        - jnp.mean(gain_applied, axis=-1, keepdims=True)
        - standardized_input * jnp.mean(gain_applied * standardized_input, axis=-1, keepdims=True)
    )
    dx_two = (d_two[0].astype(jnp.float32) + lower_gradient).astype(jnp.bfloat16)
    qkv_term = (
        lax.dot_general(
            normed_rows, d_projected, (((0,), (0,)), ((), ())), preferred_element_type=jnp.float32
        )
        * grad_scale
    )
    column_qkv = lax.psum_scatter(
        qkv_term.astype(jnp.bfloat16), "seq", scatter_dimension=1, tiled=True
    ).astype(jnp.float32)
    grad_qkv = lax.psum_scatter(column_qkv, "dp", scatter_dimension=0, tiled=True)
    return (x_one[None], dx_two[None], grad_qkv)


AXES = ("dp", "seq")
OVER_Y, OVER_CORE, OVER_X, OVER_Z1, OVER_Z2 = 1, 2, 4, 8, 16

D = 576
HALF = 288
HEAD = 72
HERE = 4
ROWS = 36
SLOT = 48
REL = 16 * SLOT
FSLOT = 208
TOK2 = 2 * FSLOT
KEYS = 128
KLANES = HERE * KEYS
QKV = 3 * HALF
SHARD = QKV + D
SEND = 640 + HALF
BF16, F32 = jnp.bfloat16, jnp.float32


def swap(array, mask):
    return lax.ppermute(array, AXES, [(i, i ^ mask) for i in range(32)])


def dot(a, b, dims=((1,), (0,))):
    return lax.dot_general(a, b, (dims, ((), ())), preferred_element_type=F32)


SLOTS = ("o", "x", "a", "xa", "b", "xb", "ab", "xab")
NT = ((1,), (1,))
TN = ((0,), (0,))


def iota(shape, dim):
    return lax.broadcasted_iota(jnp.int32, shape, dim)


def feature_of_slot(shape, dim):
    me = lax.axis_index("dp")
    at = iota(shape, dim)
    feature = jnp.full(shape, -1, jnp.int32)
    for s in range(16):
        rel = ((s & 7) << 1) | (s >> 3)
        here = (at >= SLOT * s) & (at < SLOT * s + ROWS)
        feature = jnp.where(here, (me ^ rel) * ROWS + at - SLOT * s, feature)
    return feature


def one_hot(hits):
    return jnp.where(hits, 1.0, 0.0).astype(BF16)


def key_of_token(shape, dim):
    at = iota(shape, dim)
    second = at >= FSLOT
    t = jnp.where(second, at - FSLOT, at)
    row = (t * 9363) >> 17
    col = t - row * SIDE
    key = (row >> 1) * PSIDE + (col >> 1) + jnp.where(second, 64, 0)
    return jnp.where(t < FRAME_TOK, key, -1)


def shard_kernel(qkv_hbm, out_hbm, own_ref, qkv_ref, out_ref, sems):
    loads = (
        pltpu.make_async_copy(qkv_hbm, qkv_ref, sems.at[0]),
        pltpu.make_async_copy(out_hbm, out_ref, sems.at[1]),
    )
    for load in loads:
        load.start()
    for load in loads:
        load.wait()
    y = lax.axis_index("seq")
    for s in range(2):

        @pl.when(y == s)
        def _():
            for part in range(3):
                at = part * D + s * HALF
                own_ref[:, part * HALF : (part + 1) * HALF] = qkv_ref[:, at : at + HALF]

    own_ref[:, QKV:] = out_ref[...]


def standardize(values):
    centered = values - jnp.mean(values, axis=-1, keepdims=True)
    inverse = lax.rsqrt(jnp.mean(centered * centered, axis=-1, keepdims=True) + 1e-05)
    return centered * inverse, inverse


def prep_kernel(own_ref, peer_ref, gain_ref, rel_ref, relt_ref, pool_ref, poolt_ref, order_ref):
    order = one_hot(iota((D, REL), 0) == feature_of_slot((1, REL), 1))
    order_t = one_hot(feature_of_slot((REL, 1), 0) == iota((REL, D), 1))
    order_ref[...] = order
    gain = gain_ref[...].reshape(1, D)
    for f, src in enumerate((own_ref, peer_ref)):
        normed = (standardize(src[...].astype(F32))[0] * gain).astype(BF16)
        normed = jnp.concatenate([normed, jnp.zeros((FSLOT - FRAME_TOK, D), BF16)], axis=0)
        rel_ref[f * FSLOT : (f + 1) * FSLOT, :] = dot(normed, order).astype(BF16)
        relt_ref[f] = dot(order_t, normed, NT).astype(BF16)
    table = one_hot(iota((KEYS, TOK2), 0) == key_of_token((1, TOK2), 1)) * BF16(0.25)
    pooled = dot(table, rel_ref[...])
    hi = pooled.astype(BF16)
    pool_ref[:KEYS, :] = hi
    pool_ref[KEYS:, :] = (pooled - hi.astype(F32)).astype(BF16)
    pooled_t = dot(relt_ref[0], table[:, :FSLOT], NT) + dot(relt_ref[1], table[:, FSLOT:], NT)
    hi_t = pooled_t.astype(BF16)
    poolt_ref[:, :KEYS] = hi_t
    poolt_ref[:, KEYS:] = (pooled_t - hi_t.astype(F32)).astype(BF16)


def head_lanes(h):
    lane = iota((1, HALF), 1)
    return (lane >= h * HEAD) & (lane < (h + 1) * HEAD)


def main_kernel(grad_scale, valid_ref, rel_ref, relt_ref, pool_ref, poolt_ref, order_ref, down_ref, dpeer_ref, *rest):
    blocks = rest[:16]
    gown_ref, goth_ref, w_ref, dq_ref, e_ref, mixed_ref, outh_ref = rest[16:23]
    cot_ref, kbig_ref, vbig_ref, s_ref, p_ref, ds_ref, g_ref = rest[23:]
    y = lax.axis_index("seq")
    scale = 1.0 / math.sqrt(HEAD)
    for s in range(16):
        w_ref[s * SLOT + 32 : (s + 1) * SLOT, :] = jnp.zeros((16, SHARD), BF16)
        w_ref[s * SLOT : s * SLOT + ROWS, :] = blocks[s][...]
    for f, src in enumerate((down_ref, dpeer_ref)):
        at = f * FSLOT
        cot_ref[at + 192 : at + FSLOT, :] = jnp.zeros((16, D), BF16)
        cot_ref[at : at + FRAME_TOK, :] = src[...]

    queries = dot(rel_ref[...], w_ref[:, :HALF]).astype(BF16)
    kv = dot(pool_ref[...], w_ref[:, 256:QKV])
    kv = kv[:KEYS] + kv[KEYS:]
    keys = kv[:, 32 : 32 + HALF].astype(BF16)
    values = kv[:, 32 + HALF :].astype(BF16)
    for h in range(HERE):
        lanes = head_lanes(h)
        kbig_ref[h * KEYS : (h + 1) * KEYS, :] = jnp.where(lanes, keys, BF16(0))
        vbig_ref[h * KEYS : (h + 1) * KEYS, :] = jnp.where(lanes, values, BF16(0))
    select = order_ref[pl.ds(pl.multiple_of(y * HALF, HALF), HALF), :]
    outh_ref[...] = dot(select, w_ref[:, QKV:]).astype(BF16)
    d_mixed = dot(cot_ref[...], outh_ref[...], NT).astype(BF16)

    s_ref[...] = dot(queries, kbig_ref[...], NT)
    key = iota((1, KEYS), 1)
    late = key >= 64
    frame = jnp.where(late, 1 - y, y)
    live = (jnp.where(late, key - 64, key) < PFRAME) & (frame < valid_ref[0])
    for h in range(HERE):
        cols = slice(h * KEYS, (h + 1) * KEYS)
        for f in range(2):
            rows = slice(f * FSLOT, (f + 1) * FSLOT)
            masked = jnp.where(live, s_ref[rows, cols] * scale, -jnp.inf)
            raised = jnp.exp(masked - jnp.max(masked, axis=-1, keepdims=True))
            p_ref[rows, cols] = (raised / jnp.sum(raised, axis=-1, keepdims=True)).astype(BF16)
    mixed_ref[...] = dot(p_ref[...], vbig_ref[...]).astype(BF16)
    s_ref[...] = dot(d_mixed, vbig_ref[...], NT)
    for h in range(HERE):
        cols = slice(h * KEYS, (h + 1) * KEYS)
        for f in range(2):
            rows = slice(f * FSLOT, (f + 1) * FSLOT)
            wide = p_ref[rows, cols].astype(F32)
            d_probs = s_ref[rows, cols]
            delta = jnp.sum(wide * d_probs, axis=-1, keepdims=True)
            ds_ref[rows, cols] = (wide * (d_probs - delta) * scale).astype(BF16)
    dq_ref[:, 256:384] = jnp.zeros((TOK2, 128), BF16)
    dq_ref[:, :HALF] = dot(ds_ref[...], kbig_ref[...]).astype(BF16)

    def by_head(big):
        return sum(jnp.where(head_lanes(h), big[h * KEYS : (h + 1) * KEYS], 0.0) for h in range(HERE))

    d_keys = by_head(dot(ds_ref[...], queries, TN)) * 0.25
    d_values = by_head(dot(p_ref[...], d_mixed, TN)) * 0.25
    e = jnp.concatenate([jnp.zeros((KEYS, 32), F32), d_keys, d_values], axis=1).astype(BF16)
    e_ref[:KEYS, :] = e
    e_ref[KEYS:, :] = e
    dq = dq_ref[...]
    g_q = dot(relt_ref[0], dq[:FSLOT]) + dot(relt_ref[1], dq[FSLOT:])
    g_kv = dot(poolt_ref[...], e_ref[...]) * 4.0
    g_ref[:, :256] = g_q[:, :256] * grad_scale
    g_ref[:, 256:384] = (g_q[:, 256:] + g_kv[:, :128]) * grad_scale
    g_ref[:, 384:] = g_kv[:, 128:] * grad_scale
    for s in range(8):
        gown_ref[s] = g_ref[s * SLOT : s * SLOT + ROWS, :].astype(BF16)
        goth_ref[s] = g_ref[(s + 8) * SLOT : (s + 8) * SLOT + ROWS, :].astype(BF16)


def cross_kernel(w_ref, dq_ref, e_ref, mixed_ref, order_ref, send_ref, dn_ref):
    spread = one_hot(key_of_token((TOK2, 1), 0) == iota((TOK2, KEYS), 1))
    d_tokens = dot(spread, e_ref[:KEYS, :]).astype(BF16)
    d_normed = dot(dq_ref[...], w_ref[:, :384], NT) + dot(d_tokens, w_ref[:, 256:QKV], NT)
    dn_ref[...] = d_normed[:FSLOT]
    peer = dot(d_normed[FSLOT:].astype(BF16), order_ref[...], NT)
    send_ref[:, :D] = peer[:FRAME_TOK].astype(BF16)
    send_ref[:, D:640] = jnp.zeros((FRAME_TOK, 640 - D), BF16)
    send_ref[:, 640:] = mixed_ref[FSLOT : FSLOT + FRAME_TOK, :]


def late_kernel(w_ref, dn_ref, order_ref, nat_ref, oth_ref):
    order = order_ref[...]
    hi = dn_ref[...].astype(BF16)
    lo = (dn_ref[...] - hi.astype(F32)).astype(BF16)
    nat_ref[...] = (dot(hi, order, NT) + dot(lo, order, NT))[:FRAME_TOK]
    other = 1 - lax.axis_index("seq")
    select = order_ref[pl.ds(pl.multiple_of(other * HALF, HALF), HALF), :]
    oth_ref[...] = dot(select, w_ref[:, QKV:]).astype(BF16)


def last_kernel(yone_ref, second_ref, dtwo_ref, gain_ref, got_ref, dn_ref, mixed_ref, outh_ref, oth_ref, x_ref, dx_ref):
    branch = dot(mixed_ref[:FRAME_TOK, :], outh_ref[...]) + dot(got_ref[:, 640:], oth_ref[...])
    x_ref[...] = (yone_ref[...].astype(F32) - branch).astype(BF16)
    xhat, inverse = standardize(second_ref[...].astype(F32))
    gained = (dn_ref[...] + got_ref[:, :D].astype(F32)) * gain_ref[...].reshape(1, D)
    lower = inverse * (
        gained
        - jnp.mean(gained, axis=-1, keepdims=True)
        - xhat * jnp.mean(gained * xhat, axis=-1, keepdims=True)
    )
    dx_ref[...] = (dtwo_ref[...].astype(F32) + lower).astype(BF16)


def split_kernel(own_ref, got_ref, *outs):
    for s in range(8):
        outs[s][...] = (own_ref[s].astype(F32) + got_ref[s].astype(F32)).astype(BF16)


def add_kernel(a_ref, b_ref, sum_ref):
    sum_ref[...] = (a_ref[...].astype(F32) + b_ref[...].astype(F32)).astype(BF16)


def sum_kernel(*refs):
    terms, (total_ref, cross_ref) = refs[:-2], refs[-2:]
    total = sum(t[...].astype(F32) for t in terms)
    total_ref[...] = total
    y = lax.axis_index("seq")

    @pl.when(y == 0)
    def _():
        cross_ref[...] = total[:, 2 * HALF :]

    @pl.when(y == 1)
    def _():
        cross_ref[...] = total[:, :HALF]


def join_kernel(total_ref, cross_ref, grad_ref):
    y = lax.axis_index("seq")
    grad_ref[:, HALF : 2 * HALF] = cross_ref[...]
    for s in range(2):

        @pl.when(y == s)
        def _():
            grad_ref[:, :HALF] = total_ref[:, s * HALF : (s + 1) * HALF]
            grad_ref[:, 2 * HALF :] = total_ref[:, (s + 1) * HALF : (s + 2) * HALF]


def shape(*dims, kind=BF16):
    return jax.ShapeDtypeStruct(dims, kind)


def call(kernel, outs, args, scratch=(), smem=0, hbm=False, flops=0, moved=0, limit=16):
    vmem = pl.BlockSpec(memory_space=pltpu.VMEM)
    source = pl.BlockSpec(memory_space=pltpu.HBM) if hbm else vmem
    return pl.pallas_call(
        kernel,
        out_shape=outs,
        in_specs=[pl.BlockSpec(memory_space=pltpu.SMEM)] * smem + [source] * (len(args) - smem),
        out_specs=jax.tree.map(lambda _: vmem, outs),
        scratch_shapes=scratch,
        compiler_params=pltpu.CompilerParams(vmem_limit_bytes=limit << 20),
        cost_estimate=pl.CostEstimate(flops=flops, bytes_accessed=moved, transcendentals=0),
    )(*args)


def paired_body(y_one, second_stream, d_one, d_two, layer_norm_gain, w_qkv, w_out, frames_valid):
    grad_scale = 1.0 / math.sqrt(lax.axis_size("dp") * 2 * FRAME_TOK)
    second, cot = second_stream[0], d_one[0]
    gain = layer_norm_gain

    own = call(
        shard_kernel,
        shape(ROWS, SHARD),
        (w_qkv, w_out),
        scratch=(
            pltpu.VMEM((ROWS, 2 * QKV), BF16),
            pltpu.VMEM((ROWS, D), BF16),
            pltpu.SemaphoreType.DMA((2,)),
        ),
        hbm=True,
        moved=400_000,
        limit=60,
    )
    by_b = swap(own, OVER_Z2)
    by_x = swap(own, OVER_X)
    by_a = swap(own, OVER_Z1)
    second_peer = swap(second, OVER_Y)
    cot_peer = swap(cot, OVER_Y)
    by_ab = swap(by_b, OVER_Z1)
    by_xb = swap(by_b, OVER_X)
    by_xa = swap(by_a, OVER_X)
    by_xab = swap(by_ab, OVER_X)
    mine = (own, by_x, by_a, by_xa, by_b, by_xb, by_ab, by_xab)
    other = tuple(swap(block, OVER_CORE) for block in mine)

    rel, rel_t, pool, pool_t, order = call(
        prep_kernel,
        (shape(TOK2, REL), shape(2, REL, FSLOT), shape(2 * KEYS, REL), shape(REL, 2 * KEYS), shape(D, REL)),
        (second, second_peer, gain),
        flops=1_200_000_000,
        moved=3_000_000,
    )
    g_own, g_oth, w_rel, d_q, e, mixed, out_own = call(
        functools.partial(main_kernel, grad_scale),
        (
            shape(8, ROWS, QKV),
            shape(8, ROWS, QKV),
            shape(REL, SHARD),
            shape(TOK2, 384),
            shape(2 * KEYS, 608),
            shape(TOK2, HALF),
            shape(HALF, D),
        ),
        (frames_valid, rel, rel_t, pool, pool_t, order, cot, cot_peer) + mine + other,
        scratch=(
            pltpu.VMEM((TOK2, D), BF16),
            pltpu.VMEM((KLANES, HALF), BF16),
            pltpu.VMEM((KLANES, HALF), BF16),
            pltpu.VMEM((TOK2, KLANES), F32),
            pltpu.VMEM((TOK2, KLANES), BF16),
            pltpu.VMEM((TOK2, KLANES), BF16),
            pltpu.VMEM((REL, QKV), F32),
        ),
        smem=1,
        flops=4_000_000_000,
        moved=8_000_000,
        limit=32,
    )

    block = shape(ROWS, QKV)

    def add(a, b):
        return call(add_kernel, block, (a, b), moved=200_000)

    chunk = call(split_kernel, (block,) * 8, (g_own, swap(g_oth, OVER_CORE)), moved=1_500_000)
    by_slot = dict(zip(SLOTS, chunk))
    terms = [by_slot["o"], swap(by_slot["x"], OVER_X)]
    for name, mask in (("ab", OVER_Z1 | OVER_Z2), ("b", OVER_Z2), ("a", OVER_Z1)):
        summed = add(by_slot[name], swap(by_slot["x" + name], OVER_X))
        terms.append(swap(summed, mask))
    total, crossing = call(
        sum_kernel,
        (shape(ROWS, QKV, kind=F32), shape(ROWS, HALF, kind=F32)),
        tuple(terms),
        moved=500_000,
    )
    crossed = swap(crossing, OVER_Y)
    grad_qkv = call(join_kernel, shape(ROWS, QKV, kind=F32), (total, crossed), moved=300_000)

    send, d_normed = call(
        cross_kernel,
        (shape(FRAME_TOK, SEND), shape(FSLOT, REL, kind=F32)),
        (w_rel, d_q, e, mixed, order),
        flops=1_200_000_000,
        moved=4_000_000,
    )
    got = swap(send, OVER_Y)
    d_normed, out_oth = call(
        late_kernel,
        (shape(FRAME_TOK, D, kind=F32), shape(HALF, D)),
        (w_rel, d_normed, order),
        flops=600_000_000,
        moved=3_000_000,
    )
    x_one, dx_two = call(
        last_kernel,
        (shape(FRAME_TOK, D), shape(FRAME_TOK, D)),
        (y_one[0], second, d_two[0], gain, got, d_normed, mixed, out_own, out_oth),
        flops=300_000_000,
        moved=3_000_000,
    )
    return (x_one[None], dx_two[None], grad_qkv)


def local_paired(*args):
    return paired_body(*args)


def solution(mesh):
    in_specs = (
        P("dp", "seq", None),
        P("dp", "seq", None),
        P("dp", "seq", None),
        P("dp", "seq", None),
        P(),
        P("dp", None),
        P("dp", None),
        P("dp"),
    )
    out_specs = (P("dp", "seq", None), P("dp", "seq", None), P("dp", "seq"))
    paired = dict(mesh.shape) == {"dp": 16, "seq": 2}
    local = local_paired if paired else local_general
    return jax.shard_map(local, mesh=mesh, in_specs=in_specs, out_specs=out_specs, check_vma=False)
```

```python
import functools
import math

import jax
import jax.numpy as jnp
from jax import lax
from jax.experimental import pallas as pl
from jax.experimental.pallas import tpu as pltpu
from jax.sharding import PartitionSpec as P

HEADS = 8
SIDE = 14
POOL = 2
PSIDE = 7
FRAME_TOK = 196
PFRAME = 49


def pool_table():
    token_ids = jnp.arange(FRAME_TOK, dtype=jnp.int32)
    pooled_ids = jnp.arange(PFRAME, dtype=jnp.int32)
    token_row = token_ids // SIDE // POOL
    token_col = token_ids % SIDE // POOL
    hits = (
        (token_row[None, :] == (pooled_ids // PSIDE)[:, None])
        & (token_col[None, :] == (pooled_ids % PSIDE)[:, None])
    ).astype(jnp.float32)
    return hits / jnp.sum(hits, axis=1, keepdims=True)


def normalize_rows(inputs):
    values = inputs.astype(jnp.float32)
    centered = values - jnp.mean(values, axis=-1, keepdims=True)
    inverse_deviation = lax.rsqrt(jnp.mean(centered * centered, axis=-1, keepdims=True) + 1e-05)
    return (centered * inverse_deviation, inverse_deviation)


def pool_rows(table, rows):
    frame_count = rows.shape[0] // FRAME_TOK
    shaped = rows.reshape(frame_count, FRAME_TOK, rows.shape[1])
    pooled = jnp.einsum("pt,ftw->fpw", table, shaped, precision=lax.Precision.HIGHEST)
    return pooled.reshape(frame_count * PFRAME, rows.shape[1])


def spread_rows(table, pooled):
    frame_count = pooled.shape[0] // PFRAME
    shaped = pooled.reshape(frame_count, PFRAME, pooled.shape[1])
    spread = jnp.einsum("pt,fpw->ftw", table, shaped, precision=lax.Precision.HIGHEST)
    return spread.reshape(frame_count * FRAME_TOK, pooled.shape[1])


def masked_softmax(scores, key_live):
    masked = jnp.where(key_live[None, None, :], scores, -jnp.inf)
    top = jnp.max(masked, axis=-1, keepdims=True)
    raised = jnp.exp(masked - top)
    return raised / jnp.sum(raised, axis=-1, keepdims=True)


def local_general(y_one, second_stream, d_one, d_two, layer_norm_gain, w_qkv, w_out, frames_valid):
    seq_count = lax.axis_size("seq")
    clip_count = lax.axis_size("dp")
    model_width = w_out.shape[1]
    tokens_here = second_stream.shape[1]
    head_width = model_width // HEADS
    full_qkv, full_out = (
        lax.all_gather(w_qkv, "dp", axis=0, tiled=True),
        lax.all_gather(w_out, "dp", axis=0, tiled=True),
    )
    table = pool_table()
    scale = 1.0 / math.sqrt(head_width)
    grad_scale = 1.0 / math.sqrt(clip_count * seq_count * tokens_here)
    upper = y_one[0]
    cot_one = d_one[0]
    standardized_input, inverse_deviation = normalize_rows(second_stream[0])
    normed_rows = (standardized_input * layer_norm_gain).astype(jnp.bfloat16)
    projected = jnp.dot(normed_rows, full_qkv, preferred_element_type=jnp.float32)
    queries = projected[:, :model_width].astype(jnp.bfloat16)
    own_pooled = pool_rows(table, projected[:, model_width:]).astype(jnp.bfloat16)
    all_pooled = lax.all_gather(own_pooled, "seq", axis=0, tiled=True)
    key_total = all_pooled.shape[0]
    key_live = jnp.arange(key_total, dtype=jnp.int32) // PFRAME < frames_valid[0]
    query_heads = queries.reshape(tokens_here, HEADS, head_width)
    key_heads = all_pooled[:, :model_width].reshape(key_total, HEADS, head_width)
    value_heads = all_pooled[:, model_width:].reshape(key_total, HEADS, head_width)
    scores = (
        jnp.einsum("nhe,mhe->hnm", query_heads, key_heads, preferred_element_type=jnp.float32)
        * scale
    )
    probs = masked_softmax(scores, key_live).astype(jnp.bfloat16)
    mixed_wide = jnp.einsum("hnm,mhe->nhe", probs, value_heads, preferred_element_type=jnp.float32)
    mixed = mixed_wide.reshape(tokens_here, model_width).astype(jnp.bfloat16)
    branch = jnp.dot(mixed, full_out, preferred_element_type=jnp.float32)
    x_one = (upper.astype(jnp.float32) - branch).astype(jnp.bfloat16)
    d_mixed = lax.dot_general(
        cot_one, full_out, (((1,), (1,)), ((), ())), preferred_element_type=jnp.float32
    ).astype(jnp.bfloat16)
    d_heads = d_mixed.reshape(tokens_here, HEADS, head_width)
    d_probs = jnp.einsum("nhe,mhe->hnm", d_heads, value_heads, preferred_element_type=jnp.float32)
    delta = jnp.einsum("nhe,nhe->hn", d_heads.astype(jnp.float32), mixed_wide)
    d_scores = (probs.astype(jnp.float32) * (d_probs - delta[:, :, None]) * scale).astype(
        jnp.bfloat16
    )
    d_queries = (
        jnp.einsum("hnm,mhe->nhe", d_scores, key_heads, preferred_element_type=jnp.float32)
        .reshape(tokens_here, model_width)
        .astype(jnp.bfloat16)
    )
    key_term = jnp.einsum(
        "hnm,nhe->mhe", d_scores, query_heads, preferred_element_type=jnp.float32
    ).reshape(key_total, model_width)
    value_term = jnp.einsum(
        "hnm,nhe->mhe", probs, d_heads, preferred_element_type=jnp.float32
    ).reshape(key_total, model_width)
    own_grads = lax.psum_scatter(
        jnp.concatenate([key_term, value_term], axis=1).astype(jnp.bfloat16),
        "seq",
        scatter_dimension=0,
        tiled=True,
    ).astype(jnp.float32)
    d_tokens = spread_rows(table, own_grads).astype(jnp.bfloat16)
    d_projected = jnp.concatenate([d_queries, d_tokens], axis=1)
    d_normed = lax.dot_general(
        d_projected, full_qkv, (((1,), (1,)), ((), ())), preferred_element_type=jnp.float32
    )
    gain_applied = d_normed * layer_norm_gain
    lower_gradient = inverse_deviation * (
        gain_applied
        - jnp.mean(gain_applied, axis=-1, keepdims=True)
        - standardized_input * jnp.mean(gain_applied * standardized_input, axis=-1, keepdims=True)
    )
    dx_two = (d_two[0].astype(jnp.float32) + lower_gradient).astype(jnp.bfloat16)
    qkv_term = (
        lax.dot_general(
            normed_rows, d_projected, (((0,), (0,)), ((), ())), preferred_element_type=jnp.float32
        )
        * grad_scale
    )
    column_qkv = lax.psum_scatter(
        qkv_term.astype(jnp.bfloat16), "seq", scatter_dimension=1, tiled=True
    ).astype(jnp.float32)
    grad_qkv = lax.psum_scatter(column_qkv, "dp", scatter_dimension=0, tiled=True)
    return (x_one[None], dx_two[None], grad_qkv)


AXES = ("dp", "seq")
OVER_Y, OVER_CORE, OVER_X, OVER_Z1, OVER_Z2 = 1, 2, 4, 8, 16

D = 576
HALF = 288
HEAD = 72
HERE = 4
ROWS = 36
SLOT = 48
REL = 16 * SLOT
FSLOT = 208
TOK2 = 2 * FSLOT
KEYS = 128
KLANES = HERE * KEYS
QKV = 3 * HALF
SHARD = QKV + D
SEND = D + HALF
BF16, F32 = jnp.bfloat16, jnp.float32


def swap(array, mask):
    return lax.ppermute(array, AXES, [(i, i ^ mask) for i in range(32)])


def dot(a, b, dims=((1,), (0,))):
    return lax.dot_general(a, b, (dims, ((), ())), preferred_element_type=F32)


NT = ((1,), (1,))
TN = ((0,), (0,))


def iota(shape, dim):
    return lax.broadcasted_iota(jnp.int32, shape, dim)


def feature_of_slot(shape, dim):
    me = lax.axis_index("dp")
    at = iota(shape, dim)
    feature = jnp.full(shape, -1, jnp.int32)
    for s in range(16):
        rel = ((s & 7) << 1) | (s >> 3)
        here = (at >= SLOT * s) & (at < SLOT * s + ROWS)
        feature = jnp.where(here, (me ^ rel) * ROWS + at - SLOT * s, feature)
    return feature


def one_hot(hits):
    return jnp.where(hits, 1.0, 0.0).astype(BF16)


def key_of_token(shape, dim):
    at = iota(shape, dim)
    second = at >= FSLOT
    t = jnp.where(second, at - FSLOT, at)
    row = (t * 9363) >> 17
    col = t - row * SIDE
    key = (row >> 1) * PSIDE + (col >> 1) + jnp.where(second, 64, 0)
    return jnp.where(t < FRAME_TOK, key, -1)


def shard_kernel(qkv_hbm, out_hbm, own_ref, qkv_ref, out_ref, sems):
    loads = (
        pltpu.make_async_copy(qkv_hbm, qkv_ref, sems.at[0]),
        pltpu.make_async_copy(out_hbm, out_ref, sems.at[1]),
    )
    for load in loads:
        load.start()
    for load in loads:
        load.wait()
    y = lax.axis_index("seq")
    for s in range(2):

        @pl.when(y == s)
        def _():
            for part in range(3):
                at = part * D + s * HALF
                own_ref[:, part * HALF : (part + 1) * HALF] = qkv_ref[:, at : at + HALF]

    own_ref[:, QKV:] = out_ref[...]


def standardize(values):
    centered = values - jnp.mean(values, axis=-1, keepdims=True)
    inverse = lax.rsqrt(jnp.mean(centered * centered, axis=-1, keepdims=True) + 1e-05)
    return centered * inverse, inverse


def warm_kernel(second_ref, gain_ref, second_out, gain_out):
    second_out[...] = second_ref[...]
    gain_out[...] = gain_ref[...]


def prep_kernel(own_ref, peer_ref, gain_ref, rel_ref, relt_ref, pool_ref, poolt_ref, order_ref):
    order = one_hot(iota((D, REL), 0) == feature_of_slot((1, REL), 1))
    order_t = one_hot(feature_of_slot((REL, 1), 0) == iota((REL, D), 1))
    order_ref[...] = order
    gain = gain_ref[...].reshape(1, D)
    for f, src in enumerate((own_ref, peer_ref)):
        normed = (standardize(src[...].astype(F32))[0] * gain).astype(BF16)
        normed = jnp.concatenate([normed, jnp.zeros((FSLOT - FRAME_TOK, D), BF16)], axis=0)
        rel_ref[f * FSLOT : (f + 1) * FSLOT, :] = dot(normed, order).astype(BF16)
        relt_ref[f] = dot(order_t, normed, NT).astype(BF16)
    table = one_hot(iota((KEYS, TOK2), 0) == key_of_token((1, TOK2), 1)) * BF16(0.25)
    pooled = dot(table, rel_ref[...])
    hi = pooled.astype(BF16)
    pool_ref[:KEYS, :] = hi
    pool_ref[KEYS:, :] = (pooled - hi.astype(F32)).astype(BF16)
    pooled_t = dot(relt_ref[0], table[:, :FSLOT], NT) + dot(relt_ref[1], table[:, FSLOT:], NT)
    hi_t = pooled_t.astype(BF16)
    poolt_ref[:, :KEYS] = hi_t
    poolt_ref[:, KEYS:] = (pooled_t - hi_t.astype(F32)).astype(BF16)


def head_lanes(h):
    lane = iota((1, HALF), 1)
    return (lane >= h * HEAD) & (lane < (h + 1) * HEAD)


def main_kernel(grad_scale, valid_ref, rel_ref, relt_ref, pool_ref, poolt_ref, order_ref, down_ref, dpeer_ref, *rest):
    blocks = rest[:16]
    gown_ref, goth_ref, w_ref, dq_ref, e_ref, mixed_ref, outh_ref = rest[16:23]
    cot_ref, kbig_ref, vbig_ref, s_ref, p_ref, ds_ref, g_ref = rest[23:]
    y = lax.axis_index("seq")
    scale = 1.0 / math.sqrt(HEAD)
    for s in range(16):
        w_ref[s * SLOT + 32 : (s + 1) * SLOT, :] = jnp.zeros((16, SHARD), BF16)
        w_ref[s * SLOT : s * SLOT + ROWS, :] = blocks[s][...]
    for f, src in enumerate((down_ref, dpeer_ref)):
        at = f * FSLOT
        cot_ref[at + 192 : at + FSLOT, :] = jnp.zeros((16, D), BF16)
        cot_ref[at : at + FRAME_TOK, :] = src[...]

    queries = dot(rel_ref[...], w_ref[:, :HALF]).astype(BF16)
    kv = dot(pool_ref[...], w_ref[:, 256:QKV])
    kv = kv[:KEYS] + kv[KEYS:]
    keys = kv[:, 32 : 32 + HALF].astype(BF16)
    values = kv[:, 32 + HALF :].astype(BF16)
    for h in range(HERE):
        lanes = head_lanes(h)
        kbig_ref[h * KEYS : (h + 1) * KEYS, :] = jnp.where(lanes, keys, BF16(0))
        vbig_ref[h * KEYS : (h + 1) * KEYS, :] = jnp.where(lanes, values, BF16(0))
    select = order_ref[pl.ds(pl.multiple_of(y * HALF, HALF), HALF), :]
    outh_ref[...] = dot(select, w_ref[:, QKV:]).astype(BF16)
    d_mixed = dot(cot_ref[...], outh_ref[...], NT).astype(BF16)

    s_ref[...] = dot(queries, kbig_ref[...], NT)
    key = iota((1, KEYS), 1)
    late = key >= 64
    frame = jnp.where(late, 1 - y, y)
    live = (jnp.where(late, key - 64, key) < PFRAME) & (frame < valid_ref[0])
    for h in range(HERE):
        cols = slice(h * KEYS, (h + 1) * KEYS)
        for f in range(2):
            rows = slice(f * FSLOT, (f + 1) * FSLOT)
            masked = jnp.where(live, s_ref[rows, cols] * scale, -jnp.inf)
            raised = jnp.exp(masked - jnp.max(masked, axis=-1, keepdims=True))
            p_ref[rows, cols] = (raised / jnp.sum(raised, axis=-1, keepdims=True)).astype(BF16)
    mixed_ref[...] = dot(p_ref[...], vbig_ref[...]).astype(BF16)
    s_ref[...] = dot(d_mixed, vbig_ref[...], NT)
    for h in range(HERE):
        cols = slice(h * KEYS, (h + 1) * KEYS)
        for f in range(2):
            rows = slice(f * FSLOT, (f + 1) * FSLOT)
            wide = p_ref[rows, cols].astype(F32)
            d_probs = s_ref[rows, cols]
            delta = jnp.sum(wide * d_probs, axis=-1, keepdims=True)
            ds_ref[rows, cols] = (wide * (d_probs - delta) * scale).astype(BF16)
    dq_ref[:, 256:384] = jnp.zeros((TOK2, 128), BF16)
    dq_ref[:, :HALF] = dot(ds_ref[...], kbig_ref[...]).astype(BF16)

    def by_head(big):
        return sum(jnp.where(head_lanes(h), big[h * KEYS : (h + 1) * KEYS], 0.0) for h in range(HERE))

    d_keys = by_head(dot(ds_ref[...], queries, TN)) * 0.25
    d_values = by_head(dot(p_ref[...], d_mixed, TN)) * 0.25
    e = jnp.concatenate([jnp.zeros((KEYS, 32), F32), d_keys, d_values], axis=1).astype(BF16)
    e_ref[:KEYS, :] = e
    e_ref[KEYS:, :] = e
    dq = dq_ref[...]
    g_q = dot(relt_ref[0], dq[:FSLOT]) + dot(relt_ref[1], dq[FSLOT:])
    g_kv = dot(poolt_ref[...], e_ref[...]) * 4.0
    g_ref[:, :256] = g_q[:, :256] * grad_scale
    g_ref[:, 256:384] = (g_q[:, 256:] + g_kv[:, :128]) * grad_scale
    g_ref[:, 384:] = g_kv[:, 128:] * grad_scale
    for s in range(8):
        gown_ref[s] = g_ref[s * SLOT : s * SLOT + ROWS, :].astype(BF16)
        goth_ref[s] = g_ref[(s + 8) * SLOT : (s + 8) * SLOT + ROWS, :].astype(BF16)


def d_normed_of(f, w_ref, dq_ref, e_ref):
    rows = slice(f * FSLOT, (f + 1) * FSLOT)
    keys = key_of_token((TOK2, 1), 0)[rows]
    d_tokens = dot(one_hot(keys == iota((FSLOT, KEYS), 1)), e_ref[:KEYS, :]).astype(BF16)
    return dot(dq_ref[rows, :], w_ref[:, :384], NT) + dot(d_tokens, w_ref[:, 256:QKV], NT)


def cross_kernel(w_ref, dq_ref, e_ref, mixed_ref, order_ref, send_ref):
    peer = dot(d_normed_of(1, w_ref, dq_ref, e_ref).astype(BF16), order_ref[...], NT)
    send_ref[:, :D] = peer[:FRAME_TOK].astype(BF16)
    send_ref[:, D:] = mixed_ref[FSLOT : FSLOT + FRAME_TOK, :]


def late_kernel(w_ref, dq_ref, e_ref, order_ref, nat_ref, oth_ref):
    order = order_ref[...]
    own = d_normed_of(0, w_ref, dq_ref, e_ref)
    hi = own.astype(BF16)
    lo = (own - hi.astype(F32)).astype(BF16)
    nat_ref[...] = (dot(hi, order, NT) + dot(lo, order, NT))[:FRAME_TOK]
    other = 1 - lax.axis_index("seq")
    select = order_ref[pl.ds(pl.multiple_of(other * HALF, HALF), HALF), :]
    oth_ref[...] = dot(select, w_ref[:, QKV:]).astype(BF16)


def last_kernel(yone_ref, second_ref, dtwo_ref, gain_ref, got_ref, dn_ref, mixed_ref, outh_ref, oth_ref, x_ref, dx_ref):
    branch = dot(mixed_ref[:FRAME_TOK, :], outh_ref[...]) + dot(got_ref[:, D:], oth_ref[...])
    x_ref[...] = (yone_ref[...].astype(F32) - branch).astype(BF16)
    xhat, inverse = standardize(second_ref[...].astype(F32))
    gained = (dn_ref[...] + got_ref[:, :D].astype(F32)) * gain_ref[...].reshape(1, D)
    lower = inverse * (
        gained
        - jnp.mean(gained, axis=-1, keepdims=True)
        - xhat * jnp.mean(gained * xhat, axis=-1, keepdims=True)
    )
    dx_ref[...] = (dtwo_ref[...].astype(F32) + lower).astype(BF16)


def split_kernel(own_ref, got_ref, kept_ref, xab_ref, xb_ref, near_ref):
    for ref, s in (
        (xab_ref, 7),
        (xb_ref, 5),
        (near_ref.at[0], 3),
        (near_ref.at[1], 1),
        (kept_ref.at[3], 6),
        (kept_ref.at[2], 4),
        (kept_ref.at[1], 2),
        (kept_ref.at[0], 0),
    ):
        ref[...] = (own_ref[s].astype(F32) + got_ref[s].astype(F32)).astype(BF16)


def store_parts(total, cross_ref, stay_ref):
    y = lax.axis_index("seq")

    @pl.when(y == 0)
    def _():
        cross_ref[...] = total[:, 2 * HALF :].astype(cross_ref.dtype)
        stay_ref[...] = total[:, : 2 * HALF].astype(stay_ref.dtype)

    @pl.when(y == 1)
    def _():
        cross_ref[...] = total[:, :HALF].astype(cross_ref.dtype)
        stay_ref[...] = total[:, HALF:].astype(stay_ref.dtype)


def add_kernel(at, kept_ref, got_ref, sum_ref):
    sum_ref[...] = (kept_ref[at].astype(F32) + got_ref[...].astype(F32)).astype(BF16)


def near_kernel(kept_ref, got_ref, a_ref, o_ref):
    a_ref[...] = (kept_ref[1].astype(F32) + got_ref[0].astype(F32)).astype(BF16)
    o_ref[...] = kept_ref[0].astype(F32) + got_ref[1].astype(F32)


def sum_kernel(o_ref, a_ref, ab_ref, b_ref, cross_ref, stay_ref):
    total = o_ref[...] + a_ref[...].astype(F32) + ab_ref[...].astype(F32) + b_ref[...].astype(F32)
    store_parts(total, cross_ref, stay_ref)


def join_kernel(crossed_ref, *refs):
    grad_ref = refs[-1]
    total = sum(term[...].astype(F32) for term in refs[:-1])
    grad_ref[:, :HALF] = total[:, :HALF]
    grad_ref[:, HALF : 2 * HALF] = crossed_ref[...].astype(F32)
    grad_ref[:, 2 * HALF :] = total[:, HALF:]


def shape(*dims, kind=BF16):
    return jax.ShapeDtypeStruct(dims, kind)


def call(kernel, outs, args, scratch=(), smem=0, hbm=False, flops=0, moved=0, limit=16 << 10):
    vmem = pl.BlockSpec(memory_space=pltpu.VMEM)
    source = pl.BlockSpec(memory_space=pltpu.HBM) if hbm else vmem
    return pl.pallas_call(
        kernel,
        out_shape=outs,
        in_specs=[pl.BlockSpec(memory_space=pltpu.SMEM)] * smem + [source] * (len(args) - smem),
        out_specs=jax.tree.map(lambda _: vmem, outs),
        scratch_shapes=scratch,
        compiler_params=pltpu.CompilerParams(vmem_limit_bytes=limit << 10),
        cost_estimate=pl.CostEstimate(flops=flops, bytes_accessed=moved, transcendentals=0),
    )(*args)


def paired_body(y_one, second_stream, d_one, d_two, layer_norm_gain, w_qkv, w_out, frames_valid):
    grad_scale = 1.0 / math.sqrt(lax.axis_size("dp") * 2 * FRAME_TOK)
    second, cot = second_stream[0], d_one[0]
    gain = layer_norm_gain

    own = call(
        shard_kernel,
        shape(ROWS, SHARD),
        (w_qkv, w_out),
        scratch=(
            pltpu.VMEM((ROWS, 2 * QKV), BF16),
            pltpu.VMEM((ROWS, D), BF16),
            pltpu.SemaphoreType.DMA((2,)),
        ),
        hbm=True,
        moved=400_000,
        limit=60 << 10,
    )
    by_b = swap(own, OVER_Z2)
    by_x = swap(own, OVER_X)
    by_a = swap(own, OVER_Z1)
    second_peer = swap(second, OVER_Y)
    cot_peer = swap(cot, OVER_Y)
    by_ab = swap(by_b, OVER_Z1)
    by_xb = swap(by_b, OVER_X)
    by_xa = swap(by_a, OVER_X)
    by_xab = swap(by_ab, OVER_X)
    mine = (own, by_x, by_a, by_xa, by_b, by_xb, by_ab, by_xab)
    other = tuple(swap(block, OVER_CORE) for block in mine)

    second_here, gain_here = call(
        warm_kernel, (shape(FRAME_TOK, D), shape(D, kind=F32)), (second, gain), moved=500_000
    )
    rel, rel_t, pool, pool_t, order = call(
        prep_kernel,
        (shape(TOK2, REL), shape(2, REL, FSLOT), shape(2 * KEYS, REL), shape(REL, 2 * KEYS), shape(D, REL)),
        (second_here, second_peer, gain_here),
        flops=1_200_000_000,
        moved=3_000_000,
    )
    g_own, g_oth, w_rel, d_q, e, mixed, out_own = call(
        functools.partial(main_kernel, grad_scale),
        (
            shape(8, ROWS, QKV),
            shape(8, ROWS, QKV),
            shape(REL, SHARD),
            shape(TOK2, 384),
            shape(2 * KEYS, 608),
            shape(TOK2, HALF),
            shape(HALF, D),
        ),
        (frames_valid, rel, rel_t, pool, pool_t, order, cot, cot_peer) + mine + other,
        scratch=(
            pltpu.VMEM((TOK2, D), BF16),
            pltpu.VMEM((KLANES, HALF), BF16),
            pltpu.VMEM((KLANES, HALF), BF16),
            pltpu.VMEM((TOK2, KLANES), F32),
            pltpu.VMEM((TOK2, KLANES), BF16),
            pltpu.VMEM((TOK2, KLANES), BF16),
            pltpu.VMEM((REL, QKV), F32),
        ),
        smem=1,
        flops=4_000_000_000,
        moved=8_000_000,
        limit=32 << 10,
    )

    block, pair = shape(ROWS, QKV), shape(2, ROWS, QKV)
    wide = shape(ROWS, QKV, kind=F32)
    kept, x_ab, x_b, near = call(
        split_kernel,
        (shape(4, ROWS, QKV), block, block, pair),
        (g_own, swap(g_oth, OVER_CORE)),
        moved=1_500_000,
    )
    got_ab, got_b = swap(x_ab, OVER_X), swap(x_b, OVER_X)
    to_ab = call(functools.partial(add_kernel, 3), block, (kept, got_ab), moved=200_000)
    to_b = call(functools.partial(add_kernel, 2), block, (kept, got_b), moved=200_000)
    to_a, here = call(near_kernel, (block, wide), (kept, swap(near, OVER_X)), moved=400_000)
    from_ab = swap(to_ab, OVER_Z1 | OVER_Z2)
    from_b = swap(to_b, OVER_Z2)
    from_a = swap(to_a, OVER_Z1)
    crossing, stay = call(
        sum_kernel,
        (shape(ROWS, HALF), shape(ROWS, 2 * HALF, kind=F32)),
        (here, from_a, from_ab, from_b),
        moved=400_000,
    )
    crossed = swap(crossing, OVER_Y)
    grad_qkv = call(join_kernel, wide, (crossed, stay), moved=300_000)

    send = call(
        cross_kernel,
        shape(FRAME_TOK, SEND),
        (w_rel, d_q, e, mixed, order),
        flops=600_000_000,
        moved=4_000_000,
    )
    got = swap(send, OVER_Y)
    d_normed, out_oth = call(
        late_kernel,
        (shape(FRAME_TOK, D, kind=F32), shape(HALF, D)),
        (w_rel, d_q, e, order),
        flops=1_000_000_000,
        moved=3_000_000,
    )
    x_one, dx_two = call(
        last_kernel,
        (shape(FRAME_TOK, D), shape(FRAME_TOK, D)),
        (y_one[0], second_here, d_two[0], gain_here, got, d_normed, mixed, out_own, out_oth),
        flops=300_000_000,
        moved=3_000_000,
    )
    return (x_one[None], dx_two[None], grad_qkv)


def local_paired(*args):
    return paired_body(*args)


def solution(mesh):
    in_specs = (
        P("dp", "seq", None),
        P("dp", "seq", None),
        P("dp", "seq", None),
        P("dp", "seq", None),
        P(),
        P("dp", None),
        P("dp", None),
        P("dp"),
    )
    out_specs = (P("dp", "seq", None), P("dp", "seq", None), P("dp", "seq"))
    paired = dict(mesh.shape) == {"dp": 16, "seq": 2}
    local = local_paired if paired else local_general
    return jax.shard_map(local, mesh=mesh, in_specs=in_specs, out_specs=out_specs, check_vma=False)
```

```python
import functools
import math

import jax
import jax.numpy as jnp
from jax import lax
from jax.experimental import pallas as pl
from jax.experimental.pallas import tpu as pltpu
from jax.sharding import PartitionSpec as P

HEADS = 8
SIDE = 14
POOL = 2
PSIDE = 7
FRAME_TOK = 196
PFRAME = 49


def pool_table():
    token_ids = jnp.arange(FRAME_TOK, dtype=jnp.int32)
    pooled_ids = jnp.arange(PFRAME, dtype=jnp.int32)
    token_row = token_ids // SIDE // POOL
    token_col = token_ids % SIDE // POOL
    hits = (
        (token_row[None, :] == (pooled_ids // PSIDE)[:, None])
        & (token_col[None, :] == (pooled_ids % PSIDE)[:, None])
    ).astype(jnp.float32)
    return hits / jnp.sum(hits, axis=1, keepdims=True)


def normalize_rows(inputs):
    values = inputs.astype(jnp.float32)
    centered = values - jnp.mean(values, axis=-1, keepdims=True)
    inverse_deviation = lax.rsqrt(jnp.mean(centered * centered, axis=-1, keepdims=True) + 1e-05)
    return (centered * inverse_deviation, inverse_deviation)


def pool_rows(table, rows):
    frame_count = rows.shape[0] // FRAME_TOK
    shaped = rows.reshape(frame_count, FRAME_TOK, rows.shape[1])
    pooled = jnp.einsum("pt,ftw->fpw", table, shaped, precision=lax.Precision.HIGHEST)
    return pooled.reshape(frame_count * PFRAME, rows.shape[1])


def spread_rows(table, pooled):
    frame_count = pooled.shape[0] // PFRAME
    shaped = pooled.reshape(frame_count, PFRAME, pooled.shape[1])
    spread = jnp.einsum("pt,fpw->ftw", table, shaped, precision=lax.Precision.HIGHEST)
    return spread.reshape(frame_count * FRAME_TOK, pooled.shape[1])


def masked_softmax(scores, key_live):
    masked = jnp.where(key_live[None, None, :], scores, -jnp.inf)
    top = jnp.max(masked, axis=-1, keepdims=True)
    raised = jnp.exp(masked - top)
    return raised / jnp.sum(raised, axis=-1, keepdims=True)


def local_general(y_one, second_stream, d_one, d_two, layer_norm_gain, w_qkv, w_out, frames_valid):
    seq_count = lax.axis_size("seq")
    clip_count = lax.axis_size("dp")
    model_width = w_out.shape[1]
    tokens_here = second_stream.shape[1]
    head_width = model_width // HEADS
    full_qkv, full_out = (
        lax.all_gather(w_qkv, "dp", axis=0, tiled=True),
        lax.all_gather(w_out, "dp", axis=0, tiled=True),
    )
    table = pool_table()
    scale = 1.0 / math.sqrt(head_width)
    grad_scale = 1.0 / math.sqrt(clip_count * seq_count * tokens_here)
    upper = y_one[0]
    cot_one = d_one[0]
    standardized_input, inverse_deviation = normalize_rows(second_stream[0])
    normed_rows = (standardized_input * layer_norm_gain).astype(jnp.bfloat16)
    projected = jnp.dot(normed_rows, full_qkv, preferred_element_type=jnp.float32)
    queries = projected[:, :model_width].astype(jnp.bfloat16)
    own_pooled = pool_rows(table, projected[:, model_width:]).astype(jnp.bfloat16)
    all_pooled = lax.all_gather(own_pooled, "seq", axis=0, tiled=True)
    key_total = all_pooled.shape[0]
    key_live = jnp.arange(key_total, dtype=jnp.int32) // PFRAME < frames_valid[0]
    query_heads = queries.reshape(tokens_here, HEADS, head_width)
    key_heads = all_pooled[:, :model_width].reshape(key_total, HEADS, head_width)
    value_heads = all_pooled[:, model_width:].reshape(key_total, HEADS, head_width)
    scores = (
        jnp.einsum("nhe,mhe->hnm", query_heads, key_heads, preferred_element_type=jnp.float32)
        * scale
    )
    probs = masked_softmax(scores, key_live).astype(jnp.bfloat16)
    mixed_wide = jnp.einsum("hnm,mhe->nhe", probs, value_heads, preferred_element_type=jnp.float32)
    mixed = mixed_wide.reshape(tokens_here, model_width).astype(jnp.bfloat16)
    branch = jnp.dot(mixed, full_out, preferred_element_type=jnp.float32)
    x_one = (upper.astype(jnp.float32) - branch).astype(jnp.bfloat16)
    d_mixed = lax.dot_general(
        cot_one, full_out, (((1,), (1,)), ((), ())), preferred_element_type=jnp.float32
    ).astype(jnp.bfloat16)
    d_heads = d_mixed.reshape(tokens_here, HEADS, head_width)
    d_probs = jnp.einsum("nhe,mhe->hnm", d_heads, value_heads, preferred_element_type=jnp.float32)
    delta = jnp.einsum("nhe,nhe->hn", d_heads.astype(jnp.float32), mixed_wide)
    d_scores = (probs.astype(jnp.float32) * (d_probs - delta[:, :, None]) * scale).astype(
        jnp.bfloat16
    )
    d_queries = (
        jnp.einsum("hnm,mhe->nhe", d_scores, key_heads, preferred_element_type=jnp.float32)
        .reshape(tokens_here, model_width)
        .astype(jnp.bfloat16)
    )
    key_term = jnp.einsum(
        "hnm,nhe->mhe", d_scores, query_heads, preferred_element_type=jnp.float32
    ).reshape(key_total, model_width)
    value_term = jnp.einsum(
        "hnm,nhe->mhe", probs, d_heads, preferred_element_type=jnp.float32
    ).reshape(key_total, model_width)
    own_grads = lax.psum_scatter(
        jnp.concatenate([key_term, value_term], axis=1).astype(jnp.bfloat16),
        "seq",
        scatter_dimension=0,
        tiled=True,
    ).astype(jnp.float32)
    d_tokens = spread_rows(table, own_grads).astype(jnp.bfloat16)
    d_projected = jnp.concatenate([d_queries, d_tokens], axis=1)
    d_normed = lax.dot_general(
        d_projected, full_qkv, (((1,), (1,)), ((), ())), preferred_element_type=jnp.float32
    )
    gain_applied = d_normed * layer_norm_gain
    lower_gradient = inverse_deviation * (
        gain_applied
        - jnp.mean(gain_applied, axis=-1, keepdims=True)
        - standardized_input * jnp.mean(gain_applied * standardized_input, axis=-1, keepdims=True)
    )
    dx_two = (d_two[0].astype(jnp.float32) + lower_gradient).astype(jnp.bfloat16)
    qkv_term = (
        lax.dot_general(
            normed_rows, d_projected, (((0,), (0,)), ((), ())), preferred_element_type=jnp.float32
        )
        * grad_scale
    )
    column_qkv = lax.psum_scatter(
        qkv_term.astype(jnp.bfloat16), "seq", scatter_dimension=1, tiled=True
    ).astype(jnp.float32)
    grad_qkv = lax.psum_scatter(column_qkv, "dp", scatter_dimension=0, tiled=True)
    return (x_one[None], dx_two[None], grad_qkv)


AXES = ("dp", "seq")
OVER_Y, OVER_CORE, OVER_X, OVER_Z1, OVER_Z2 = 1, 2, 4, 8, 16

D = 576
HALF = 288
HEAD = 72
HERE = 4
ROWS = 36
SLOT = 48
REL = 16 * SLOT
FSLOT = 208
TOK2 = 2 * FSLOT
KEYS = 128
KLANES = HERE * KEYS
QKV = 3 * HALF
SHARD = QKV + D
LOW = 512
EARLY = 11
SEND = D + HALF
BF16, F32 = jnp.bfloat16, jnp.float32


def swap(array, mask):
    return lax.ppermute(array, AXES, [(i, i ^ mask) for i in range(32)])


def dot(a, b, dims=((1,), (0,))):
    return lax.dot_general(a, b, (dims, ((), ())), preferred_element_type=F32)


NT = ((1,), (1,))
TN = ((0,), (0,))


def iota(shape, dim):
    return lax.broadcasted_iota(jnp.int32, shape, dim)


def feature_of_slot(shape, dim):
    me = lax.axis_index("dp")
    at = iota(shape, dim)
    feature = jnp.full(shape, -1, jnp.int32)
    for s in range(16):
        rel = ((s & 7) << 1) | (s >> 3)
        here = (at >= SLOT * s) & (at < SLOT * s + ROWS)
        feature = jnp.where(here, (me ^ rel) * ROWS + at - SLOT * s, feature)
    return feature


def one_hot(hits):
    return jnp.where(hits, 1.0, 0.0).astype(BF16)


def key_of_token(shape, dim):
    at = iota(shape, dim)
    second = at >= FSLOT
    t = jnp.where(second, at - FSLOT, at)
    row = (t * 9363) >> 17
    col = t - row * SIDE
    key = (row >> 1) * PSIDE + (col >> 1) + jnp.where(second, 64, 0)
    return jnp.where(t < FRAME_TOK, key, -1)


def shard_kernel(qkv_hbm, out_hbm, own_ref, qkv_ref, out_ref, sems):
    loads = (
        pltpu.make_async_copy(qkv_hbm, qkv_ref, sems.at[0]),
        pltpu.make_async_copy(out_hbm, out_ref, sems.at[1]),
    )
    for load in loads:
        load.start()
    for load in loads:
        load.wait()
    y = lax.axis_index("seq")
    for s in range(2):

        @pl.when(y == s)
        def _():
            for part in range(3):
                at = part * D + s * HALF
                own_ref[:, part * HALF : (part + 1) * HALF] = qkv_ref[:, at : at + HALF]

    own_ref[:, QKV:] = out_ref[...]


def standardize(values):
    centered = values - jnp.mean(values, axis=-1, keepdims=True)
    inverse = lax.rsqrt(jnp.mean(centered * centered, axis=-1, keepdims=True) + 1e-05)
    return centered * inverse, inverse


def warm_kernel(second_ref, gain_ref, second_out, gain_out):
    second_out[...] = second_ref[...]
    gain_out[...] = gain_ref[...]


def prep_kernel(own_ref, peer_ref, gain_ref, rel_ref, relt_ref, pool_ref, poolt_ref, order_ref):
    order = one_hot(iota((D, REL), 0) == feature_of_slot((1, REL), 1))
    order_t = one_hot(feature_of_slot((REL, 1), 0) == iota((REL, D), 1))
    order_ref[...] = order
    gain = gain_ref[...].reshape(1, D)
    for f, src in enumerate((own_ref, peer_ref)):
        normed = (standardize(src[...].astype(F32))[0] * gain).astype(BF16)
        normed = jnp.concatenate([normed, jnp.zeros((FSLOT - FRAME_TOK, D), BF16)], axis=0)
        rel_ref[f * FSLOT : (f + 1) * FSLOT, :] = dot(normed, order).astype(BF16)
        relt_ref[f] = dot(order_t, normed, NT).astype(BF16)
    table = one_hot(iota((KEYS, TOK2), 0) == key_of_token((1, TOK2), 1)) * BF16(0.25)
    pooled = dot(table, rel_ref[...])
    hi = pooled.astype(BF16)
    pool_ref[:KEYS, :] = hi
    pool_ref[KEYS:, :] = (pooled - hi.astype(F32)).astype(BF16)
    pooled_t = dot(relt_ref[0], table[:, :FSLOT], NT) + dot(relt_ref[1], table[:, FSLOT:], NT)
    hi_t = pooled_t.astype(BF16)
    poolt_ref[:, :KEYS] = hi_t
    poolt_ref[:, KEYS:] = (pooled_t - hi_t.astype(F32)).astype(BF16)


def head_lanes(h):
    lane = iota((1, HALF), 1)
    return (lane >= h * HEAD) & (lane < (h + 1) * HEAD)


def pre_kernel(rel_ref, pool_ref, order_ref, *rest):
    blocks, (w_ref, q_ref, kv_ref, sel_ref) = rest[:EARLY], rest[EARLY:]
    for s in range(EARLY):
        at = s * SLOT
        if s < EARLY - 1:
            w_ref[at + 32 : at + SLOT, :] = jnp.zeros((16, SHARD), BF16)
            w_ref[at : at + ROWS, :] = blocks[s][...]
        else:
            w_ref[at:LOW, :] = blocks[s][: LOW - at, :]
    q_ref[...] = dot(rel_ref[:, :LOW], w_ref[:, :HALF])
    kv_ref[...] = dot(pool_ref[:, :LOW], w_ref[:, 256:QKV])
    first = pl.multiple_of(lax.axis_index("seq") * HALF, HALF)
    sel_ref[...] = dot(order_ref[pl.ds(first, HALF), :LOW], w_ref[:, QKV:])


def weight_grads(half, grad_scale, relt_ref, poolt_ref, dq_ref, e_ref, g_ref, out_ref):
    rows = slice(half * 8 * SLOT, (half + 1) * 8 * SLOT)
    g_q = dot(relt_ref[0, rows, :], dq_ref[:FSLOT, :]) + dot(relt_ref[1, rows, :], dq_ref[FSLOT:, :])
    g_kv = dot(poolt_ref[rows, :], e_ref[...]) * 4.0
    g_ref[:, :256] = g_q[:, :256] * grad_scale
    g_ref[:, 256:384] = (g_q[:, 256:] + g_kv[:, :128]) * grad_scale
    g_ref[:, 384:] = g_kv[:, 128:] * grad_scale
    for s in range(8):
        out_ref[s] = g_ref[s * SLOT : s * SLOT + ROWS, :].astype(BF16)


def own_kernel(grad_scale, relt_ref, poolt_ref, dq_ref, e_ref, out_ref, g_ref):
    weight_grads(0, grad_scale, relt_ref, poolt_ref, dq_ref, e_ref, g_ref, out_ref)


def main_kernel(grad_scale, valid_ref, rel_ref, relt_ref, pool_ref, poolt_ref, order_ref, down_ref, dpeer_ref, *rest):
    q_ref, kv_ref, sel_ref = rest[:3]
    blocks, rest = rest[3 : 20 - EARLY], rest[20 - EARLY :]
    goth_ref, w_ref, dq_ref, e_ref, mixed_ref, outh_ref = rest[:6]
    cot_ref, kbig_ref, vbig_ref, s_ref, p_ref, ds_ref, g_ref = rest[6:]
    y = lax.axis_index("seq")
    scale = 1.0 / math.sqrt(HEAD)
    straddle = LOW - (EARLY - 1) * SLOT
    w_ref[:16, :] = jnp.zeros((16, SHARD), BF16)
    w_ref[: ROWS - straddle, :] = blocks[0][straddle:, :]
    for s in range(EARLY, 16):
        at = s * SLOT - LOW
        w_ref[at + 32 : at + SLOT, :] = jnp.zeros((16, SHARD), BF16)
        w_ref[at : at + ROWS, :] = blocks[s - EARLY + 1][...]
    for f, src in enumerate((down_ref, dpeer_ref)):
        at = f * FSLOT
        cot_ref[at + 192 : at + FSLOT, :] = jnp.zeros((16, D), BF16)
        cot_ref[at : at + FRAME_TOK, :] = src[...]

    queries = (q_ref[...] + dot(rel_ref[:, LOW:], w_ref[:, :HALF])).astype(BF16)
    kv = kv_ref[...] + dot(pool_ref[:, LOW:], w_ref[:, 256:QKV])
    kv = kv[:KEYS] + kv[KEYS:]
    keys = kv[:, 32 : 32 + HALF].astype(BF16)
    values = kv[:, 32 + HALF :].astype(BF16)
    for h in range(HERE):
        lanes = head_lanes(h)
        kbig_ref[h * KEYS : (h + 1) * KEYS, :] = jnp.where(lanes, keys, BF16(0))
        vbig_ref[h * KEYS : (h + 1) * KEYS, :] = jnp.where(lanes, values, BF16(0))
    select = order_ref[pl.ds(pl.multiple_of(y * HALF, HALF), HALF), LOW:]
    outh_ref[...] = (sel_ref[...] + dot(select, w_ref[:, QKV:])).astype(BF16)
    d_mixed = dot(cot_ref[...], outh_ref[...], NT).astype(BF16)

    s_ref[...] = dot(queries, kbig_ref[...], NT)
    key = iota((1, KEYS), 1)
    late = key >= 64
    frame = jnp.where(late, 1 - y, y)
    live = (jnp.where(late, key - 64, key) < PFRAME) & (frame < valid_ref[0])
    for h in range(HERE):
        cols = slice(h * KEYS, (h + 1) * KEYS)
        for f in range(2):
            rows = slice(f * FSLOT, (f + 1) * FSLOT)
            masked = jnp.where(live, s_ref[rows, cols] * scale, -jnp.inf)
            raised = jnp.exp(masked - jnp.max(masked, axis=-1, keepdims=True))
            p_ref[rows, cols] = (raised / jnp.sum(raised, axis=-1, keepdims=True)).astype(BF16)
    mixed_ref[...] = dot(p_ref[...], vbig_ref[...]).astype(BF16)
    s_ref[...] = dot(d_mixed, vbig_ref[...], NT)
    for h in range(HERE):
        cols = slice(h * KEYS, (h + 1) * KEYS)
        for f in range(2):
            rows = slice(f * FSLOT, (f + 1) * FSLOT)
            wide = p_ref[rows, cols].astype(F32)
            d_probs = s_ref[rows, cols]
            delta = jnp.sum(wide * d_probs, axis=-1, keepdims=True)
            ds_ref[rows, cols] = (wide * (d_probs - delta) * scale).astype(BF16)
    dq_ref[:, 256:384] = jnp.zeros((TOK2, 128), BF16)
    dq_ref[:, :HALF] = dot(ds_ref[...], kbig_ref[...]).astype(BF16)

    def by_head(big):
        return sum(jnp.where(head_lanes(h), big[h * KEYS : (h + 1) * KEYS], 0.0) for h in range(HERE))

    d_keys = by_head(dot(ds_ref[...], queries, TN)) * 0.25
    d_values = by_head(dot(p_ref[...], d_mixed, TN)) * 0.25
    e = jnp.concatenate([jnp.zeros((KEYS, 32), F32), d_keys, d_values], axis=1).astype(BF16)
    e_ref[:KEYS, :] = e
    e_ref[KEYS:, :] = e
    weight_grads(1, grad_scale, relt_ref, poolt_ref, dq_ref, e_ref, g_ref, goth_ref)


def d_normed_of(f, low_ref, high_ref, dq_ref, e_ref):
    rows = slice(f * FSLOT, (f + 1) * FSLOT)
    keys = key_of_token((TOK2, 1), 0)[rows]
    d_tokens = dot(one_hot(keys == iota((FSLOT, KEYS), 1)), e_ref[:KEYS, :]).astype(BF16)
    d_queries = dq_ref[rows, :]
    return jnp.concatenate(
        [dot(d_queries, w[:, :384], NT) + dot(d_tokens, w[:, 256:QKV], NT) for w in (low_ref, high_ref)], axis=1
    )


def cross_kernel(low_ref, high_ref, dq_ref, e_ref, mixed_ref, order_ref, send_ref):
    peer = dot(d_normed_of(1, low_ref, high_ref, dq_ref, e_ref).astype(BF16), order_ref[...], NT)
    send_ref[:, :D] = peer[:FRAME_TOK].astype(BF16)
    send_ref[:, D:] = mixed_ref[FSLOT : FSLOT + FRAME_TOK, :]


def late_kernel(low_ref, high_ref, dq_ref, e_ref, order_ref, nat_ref, oth_ref):
    order = order_ref[...]
    own = d_normed_of(0, low_ref, high_ref, dq_ref, e_ref).astype(BF16)
    nat_ref[...] = dot(own, order, NT)[:FRAME_TOK].astype(BF16)
    other = 1 - lax.axis_index("seq")
    select = order_ref[pl.ds(pl.multiple_of(other * HALF, HALF), HALF), :]
    oth_ref[...] = (dot(select[:, :LOW], low_ref[:, QKV:]) + dot(select[:, LOW:], high_ref[:, QKV:])).astype(BF16)


def last_kernel(yone_ref, second_ref, dtwo_ref, gain_ref, got_ref, dn_ref, mixed_ref, outh_ref, oth_ref, x_ref, dx_ref):
    branch = dot(mixed_ref[:FRAME_TOK, :], outh_ref[...]) + dot(got_ref[:, D:], oth_ref[...])
    x_ref[...] = (yone_ref[...].astype(F32) - branch).astype(BF16)
    xhat, inverse = standardize(second_ref[...].astype(F32))
    gained = (dn_ref[...].astype(F32) + got_ref[:, :D].astype(F32)) * gain_ref[...].reshape(1, D)
    lower = inverse * (
        gained
        - jnp.mean(gained, axis=-1, keepdims=True)
        - xhat * jnp.mean(gained * xhat, axis=-1, keepdims=True)
    )
    dx_ref[...] = (dtwo_ref[...].astype(F32) + lower).astype(BF16)


def split_kernel(own_ref, got_ref, kept_ref, xab_ref, xb_ref, near_ref):
    for ref, s in (
        (xab_ref, 7),
        (xb_ref, 5),
        (near_ref.at[0], 3),
        (near_ref.at[1], 1),
        (kept_ref.at[3], 6),
        (kept_ref.at[2], 4),
        (kept_ref.at[1], 2),
        (kept_ref.at[0], 0),
    ):
        ref[...] = (own_ref[s].astype(F32) + got_ref[s].astype(F32)).astype(BF16)


def store_parts(total, cross_ref, stay_ref):
    y = lax.axis_index("seq")

    @pl.when(y == 0)
    def _():
        cross_ref[...] = total[:, 2 * HALF :].astype(cross_ref.dtype)
        stay_ref[...] = total[:, : 2 * HALF].astype(stay_ref.dtype)

    @pl.when(y == 1)
    def _():
        cross_ref[...] = total[:, :HALF].astype(cross_ref.dtype)
        stay_ref[...] = total[:, HALF:].astype(stay_ref.dtype)


def add_kernel(at, kept_ref, got_ref, sum_ref):
    sum_ref[...] = (kept_ref[at].astype(F32) + got_ref[...].astype(F32)).astype(BF16)


def part_kernel(at, kept_ref, got_ref, cross_ref, stay_ref):
    store_parts(kept_ref[at].astype(F32) + got_ref[...].astype(F32), cross_ref, stay_ref)


def near_kernel(kept_ref, got_ref, a_ref, o_ref):
    a_ref[...] = (kept_ref[1].astype(F32) + got_ref[0].astype(F32)).astype(BF16)
    o_ref[...] = kept_ref[0].astype(F32) + got_ref[1].astype(F32)


def sum_kernel(o_ref, a_ref, ab_ref, b_ref, cross_ref, stay_ref):
    total = o_ref[...] + a_ref[...].astype(F32) + ab_ref[...].astype(F32)
    y = lax.axis_index("seq")

    @pl.when(y == 0)
    def _():
        cross_ref[...] = (total[:, 2 * HALF :] + b_ref[...].astype(F32)).astype(BF16)
        stay_ref[...] = total[:, : 2 * HALF]

    @pl.when(y == 1)
    def _():
        cross_ref[...] = (total[:, :HALF] + b_ref[...].astype(F32)).astype(BF16)
        stay_ref[...] = total[:, HALF:]


def join_kernel(crossed_ref, *refs):
    grad_ref = refs[-1]
    total = sum(term[...].astype(F32) for term in refs[:-1])
    grad_ref[:, :HALF] = total[:, :HALF]
    grad_ref[:, HALF : 2 * HALF] = crossed_ref[...].astype(F32)
    grad_ref[:, 2 * HALF :] = total[:, HALF:]


def shape(*dims, kind=BF16):
    return jax.ShapeDtypeStruct(dims, kind)


def call(kernel, outs, args, scratch=(), smem=0, hbm=False, flops=0, moved=0, limit=16 << 10):
    vmem = pl.BlockSpec(memory_space=pltpu.VMEM)
    source = pl.BlockSpec(memory_space=pltpu.HBM) if hbm else vmem
    return pl.pallas_call(
        kernel,
        out_shape=outs,
        in_specs=[pl.BlockSpec(memory_space=pltpu.SMEM)] * smem + [source] * (len(args) - smem),
        out_specs=jax.tree.map(lambda _: vmem, outs),
        scratch_shapes=scratch,
        compiler_params=pltpu.CompilerParams(vmem_limit_bytes=limit << 10),
        cost_estimate=pl.CostEstimate(flops=flops, bytes_accessed=moved, transcendentals=0),
    )(*args)


def paired_body(y_one, second_stream, d_one, d_two, layer_norm_gain, w_qkv, w_out, frames_valid):
    grad_scale = 1.0 / math.sqrt(lax.axis_size("dp") * 2 * FRAME_TOK)
    second, cot = second_stream[0], d_one[0]
    gain = layer_norm_gain

    own = call(
        shard_kernel,
        shape(ROWS, SHARD),
        (w_qkv, w_out),
        scratch=(
            pltpu.VMEM((ROWS, 2 * QKV), BF16),
            pltpu.VMEM((ROWS, D), BF16),
            pltpu.SemaphoreType.DMA((2,)),
        ),
        hbm=True,
        moved=400_000,
        limit=60 << 10,
    )
    by_b = swap(own, OVER_Z2)
    by_x = swap(own, OVER_X)
    by_a = swap(own, OVER_Z1)
    second_peer = swap(second, OVER_Y)
    cot_peer = swap(cot, OVER_Y)
    by_ab = swap(by_b, OVER_Z1)
    by_xb = swap(by_b, OVER_X)
    by_xa = swap(by_a, OVER_X)
    by_xab = swap(by_ab, OVER_X)
    mine = (own, by_x, by_a, by_xa, by_b, by_xb, by_ab, by_xab)
    other = tuple(swap(block, OVER_CORE) for block in mine)

    second_here, gain_here = call(
        warm_kernel, (shape(FRAME_TOK, D), shape(D, kind=F32)), (second, gain), moved=500_000
    )
    rel, rel_t, pool, pool_t, order = call(
        prep_kernel,
        (shape(TOK2, REL), shape(2, REL, FSLOT), shape(2 * KEYS, REL), shape(REL, 2 * KEYS), shape(D, REL)),
        (second_here, second_peer, gain_here),
        flops=1_200_000_000,
        moved=3_000_000,
    )
    blocks = mine + other
    w_low, q_low, kv_low, sel_low = call(
        pre_kernel,
        (
            shape(LOW, SHARD),
            shape(TOK2, HALF, kind=F32),
            shape(2 * KEYS, 608, kind=F32),
            shape(HALF, D, kind=F32),
        ),
        (rel, pool, order) + blocks[:EARLY],
        flops=800_000_000,
        moved=4_000_000,
    )
    g_oth, w_high, d_q, e, mixed, out_own = call(
        functools.partial(main_kernel, grad_scale),
        (
            shape(8, ROWS, QKV),
            shape(REL - LOW, SHARD),
            shape(TOK2, 384),
            shape(2 * KEYS, 608),
            shape(TOK2, HALF),
            shape(HALF, D),
        ),
        (frames_valid, rel, rel_t, pool, pool_t, order, cot, cot_peer, q_low, kv_low, sel_low) + blocks[EARLY - 1 :],
        scratch=(
            pltpu.VMEM((TOK2, D), BF16),
            pltpu.VMEM((KLANES, HALF), BF16),
            pltpu.VMEM((KLANES, HALF), BF16),
            pltpu.VMEM((TOK2, KLANES), F32),
            pltpu.VMEM((TOK2, KLANES), BF16),
            pltpu.VMEM((TOK2, KLANES), BF16),
            pltpu.VMEM((8 * SLOT, QKV), F32),
        ),
        smem=1,
        flops=4_000_000_000,
        moved=8_000_000,
        limit=32 << 10,
    )

    g_own = call(
        functools.partial(own_kernel, grad_scale),
        shape(8, ROWS, QKV),
        (rel_t, pool_t, d_q, e),
        scratch=(pltpu.VMEM((8 * SLOT, QKV), F32),),
        flops=500_000_000,
        moved=2_000_000,
    )
    block, pair = shape(ROWS, QKV), shape(2, ROWS, QKV)
    wide = shape(ROWS, QKV, kind=F32)
    kept, x_ab, x_b, near = call(
        split_kernel,
        (shape(4, ROWS, QKV), block, block, pair),
        (g_own, swap(g_oth, OVER_CORE)),
        moved=1_500_000,
    )
    got_ab, got_b = swap(x_ab, OVER_X), swap(x_b, OVER_X)
    to_ab = call(functools.partial(add_kernel, 3), block, (kept, got_ab), moved=200_000)
    to_b = call(
        functools.partial(part_kernel, 2),
        (shape(ROWS, HALF), shape(ROWS, 2 * HALF)),
        (kept, got_b),
        moved=200_000,
    )
    to_a, here = call(near_kernel, (block, wide), (kept, swap(near, OVER_X)), moved=400_000)
    from_ab = swap(to_ab, OVER_Z1 | OVER_Z2)
    from_b, from_b_stay = swap(to_b[0], OVER_Z2), swap(to_b[1], OVER_Z2)
    from_a = swap(to_a, OVER_Z1)
    crossing, stay = call(
        sum_kernel,
        (shape(ROWS, HALF), shape(ROWS, 2 * HALF, kind=F32)),
        (here, from_a, from_ab, from_b),
        moved=400_000,
    )
    crossed = swap(crossing, OVER_Y)
    grad_qkv = call(join_kernel, wide, (crossed, stay, from_b_stay), moved=300_000)

    send = call(
        cross_kernel,
        shape(FRAME_TOK, SEND),
        (w_low, w_high, d_q, e, mixed, order),
        flops=600_000_000,
        moved=4_000_000,
    )
    got = swap(send, OVER_Y)
    d_normed, out_oth = call(
        late_kernel,
        (shape(FRAME_TOK, D), shape(HALF, D)),
        (w_low, w_high, d_q, e, order),
        flops=1_000_000_000,
        moved=3_000_000,
    )
    x_one, dx_two = call(
        last_kernel,
        (shape(FRAME_TOK, D), shape(FRAME_TOK, D)),
        (y_one[0], second_here, d_two[0], gain_here, got, d_normed, mixed, out_own, out_oth),
        flops=300_000_000,
        moved=3_000_000,
    )
    return (x_one[None], dx_two[None], grad_qkv)


def local_paired(*args):
    return paired_body(*args)


def solution(mesh):
    in_specs = (
        P("dp", "seq", None),
        P("dp", "seq", None),
        P("dp", "seq", None),
        P("dp", "seq", None),
        P(),
        P("dp", None),
        P("dp", None),
        P("dp"),
    )
    out_specs = (P("dp", "seq", None), P("dp", "seq", None), P("dp", "seq"))
    paired = dict(mesh.shape) == {"dp": 16, "seq": 2}
    local = local_paired if paired else local_general
    return jax.shard_map(local, mesh=mesh, in_specs=in_specs, out_specs=out_specs, check_vma=False)
```

```python
import functools
import math

import jax
import jax.numpy as jnp
from jax import lax
from jax.experimental import pallas as pl
from jax.experimental.pallas import tpu as pltpu
from jax.sharding import PartitionSpec as P

HEADS = 8
SIDE = 14
POOL = 2
PSIDE = 7
FRAME_TOK = 196
PFRAME = 49


def pool_table():
    token_ids = jnp.arange(FRAME_TOK, dtype=jnp.int32)
    pooled_ids = jnp.arange(PFRAME, dtype=jnp.int32)
    token_row = token_ids // SIDE // POOL
    token_col = token_ids % SIDE // POOL
    hits = (
        (token_row[None, :] == (pooled_ids // PSIDE)[:, None])
        & (token_col[None, :] == (pooled_ids % PSIDE)[:, None])
    ).astype(jnp.float32)
    return hits / jnp.sum(hits, axis=1, keepdims=True)


def normalize_rows(inputs):
    values = inputs.astype(jnp.float32)
    centered = values - jnp.mean(values, axis=-1, keepdims=True)
    inverse_deviation = lax.rsqrt(jnp.mean(centered * centered, axis=-1, keepdims=True) + 1e-05)
    return (centered * inverse_deviation, inverse_deviation)


def pool_rows(table, rows):
    frame_count = rows.shape[0] // FRAME_TOK
    shaped = rows.reshape(frame_count, FRAME_TOK, rows.shape[1])
    pooled = jnp.einsum("pt,ftw->fpw", table, shaped, precision=lax.Precision.HIGHEST)
    return pooled.reshape(frame_count * PFRAME, rows.shape[1])


def spread_rows(table, pooled):
    frame_count = pooled.shape[0] // PFRAME
    shaped = pooled.reshape(frame_count, PFRAME, pooled.shape[1])
    spread = jnp.einsum("pt,fpw->ftw", table, shaped, precision=lax.Precision.HIGHEST)
    return spread.reshape(frame_count * FRAME_TOK, pooled.shape[1])


def masked_softmax(scores, key_live):
    masked = jnp.where(key_live[None, None, :], scores, -jnp.inf)
    top = jnp.max(masked, axis=-1, keepdims=True)
    raised = jnp.exp(masked - top)
    return raised / jnp.sum(raised, axis=-1, keepdims=True)


def local_general(y_one, second_stream, d_one, d_two, layer_norm_gain, w_qkv, w_out, frames_valid):
    seq_count = lax.axis_size("seq")
    clip_count = lax.axis_size("dp")
    model_width = w_out.shape[1]
    tokens_here = second_stream.shape[1]
    head_width = model_width // HEADS
    full_qkv, full_out = (
        lax.all_gather(w_qkv, "dp", axis=0, tiled=True),
        lax.all_gather(w_out, "dp", axis=0, tiled=True),
    )
    table = pool_table()
    scale = 1.0 / math.sqrt(head_width)
    grad_scale = 1.0 / math.sqrt(clip_count * seq_count * tokens_here)
    upper = y_one[0]
    cot_one = d_one[0]
    standardized_input, inverse_deviation = normalize_rows(second_stream[0])
    normed_rows = (standardized_input * layer_norm_gain).astype(jnp.bfloat16)
    projected = jnp.dot(normed_rows, full_qkv, preferred_element_type=jnp.float32)
    queries = projected[:, :model_width].astype(jnp.bfloat16)
    own_pooled = pool_rows(table, projected[:, model_width:]).astype(jnp.bfloat16)
    all_pooled = lax.all_gather(own_pooled, "seq", axis=0, tiled=True)
    key_total = all_pooled.shape[0]
    key_live = jnp.arange(key_total, dtype=jnp.int32) // PFRAME < frames_valid[0]
    query_heads = queries.reshape(tokens_here, HEADS, head_width)
    key_heads = all_pooled[:, :model_width].reshape(key_total, HEADS, head_width)
    value_heads = all_pooled[:, model_width:].reshape(key_total, HEADS, head_width)
    scores = (
        jnp.einsum("nhe,mhe->hnm", query_heads, key_heads, preferred_element_type=jnp.float32)
        * scale
    )
    probs = masked_softmax(scores, key_live).astype(jnp.bfloat16)
    mixed_wide = jnp.einsum("hnm,mhe->nhe", probs, value_heads, preferred_element_type=jnp.float32)
    mixed = mixed_wide.reshape(tokens_here, model_width).astype(jnp.bfloat16)
    branch = jnp.dot(mixed, full_out, preferred_element_type=jnp.float32)
    x_one = (upper.astype(jnp.float32) - branch).astype(jnp.bfloat16)
    d_mixed = lax.dot_general(
        cot_one, full_out, (((1,), (1,)), ((), ())), preferred_element_type=jnp.float32
    ).astype(jnp.bfloat16)
    d_heads = d_mixed.reshape(tokens_here, HEADS, head_width)
    d_probs = jnp.einsum("nhe,mhe->hnm", d_heads, value_heads, preferred_element_type=jnp.float32)
    delta = jnp.einsum("nhe,nhe->hn", d_heads.astype(jnp.float32), mixed_wide)
    d_scores = (probs.astype(jnp.float32) * (d_probs - delta[:, :, None]) * scale).astype(
        jnp.bfloat16
    )
    d_queries = (
        jnp.einsum("hnm,mhe->nhe", d_scores, key_heads, preferred_element_type=jnp.float32)
        .reshape(tokens_here, model_width)
        .astype(jnp.bfloat16)
    )
    key_term = jnp.einsum(
        "hnm,nhe->mhe", d_scores, query_heads, preferred_element_type=jnp.float32
    ).reshape(key_total, model_width)
    value_term = jnp.einsum(
        "hnm,nhe->mhe", probs, d_heads, preferred_element_type=jnp.float32
    ).reshape(key_total, model_width)
    own_grads = lax.psum_scatter(
        jnp.concatenate([key_term, value_term], axis=1).astype(jnp.bfloat16),
        "seq",
        scatter_dimension=0,
        tiled=True,
    ).astype(jnp.float32)
    d_tokens = spread_rows(table, own_grads).astype(jnp.bfloat16)
    d_projected = jnp.concatenate([d_queries, d_tokens], axis=1)
    d_normed = lax.dot_general(
        d_projected, full_qkv, (((1,), (1,)), ((), ())), preferred_element_type=jnp.float32
    )
    gain_applied = d_normed * layer_norm_gain
    lower_gradient = inverse_deviation * (
        gain_applied
        - jnp.mean(gain_applied, axis=-1, keepdims=True)
        - standardized_input * jnp.mean(gain_applied * standardized_input, axis=-1, keepdims=True)
    )
    dx_two = (d_two[0].astype(jnp.float32) + lower_gradient).astype(jnp.bfloat16)
    qkv_term = (
        lax.dot_general(
            normed_rows, d_projected, (((0,), (0,)), ((), ())), preferred_element_type=jnp.float32
        )
        * grad_scale
    )
    column_qkv = lax.psum_scatter(
        qkv_term.astype(jnp.bfloat16), "seq", scatter_dimension=1, tiled=True
    ).astype(jnp.float32)
    grad_qkv = lax.psum_scatter(column_qkv, "dp", scatter_dimension=0, tiled=True)
    return (x_one[None], dx_two[None], grad_qkv)


AXES = ("dp", "seq")
OVER_Y, OVER_CORE, OVER_X, OVER_Z1, OVER_Z2 = 1, 2, 4, 8, 16

D = 576
HALF = 288
HEAD = 72
HERE = 4
ROWS = 36
SLOT = 48
REL = 16 * SLOT
FSLOT = 208
TOK2 = 2 * FSLOT
KEYS = 128
KLANES = HERE * KEYS
QKV = 3 * HALF
SHARD = QKV + D
LOW = 512
EARLY = 11
SEND = D + HALF
BF16, F32 = jnp.bfloat16, jnp.float32


def swap(array, mask):
    return lax.ppermute(array, AXES, [(i, i ^ mask) for i in range(32)])


def dot(a, b, dims=((1,), (0,))):
    return lax.dot_general(a, b, (dims, ((), ())), preferred_element_type=F32)


NT = ((1,), (1,))
TN = ((0,), (0,))


def iota(shape, dim):
    return lax.broadcasted_iota(jnp.int32, shape, dim)


def feature_of_slot(shape, dim):
    me = lax.axis_index("dp")
    at = iota(shape, dim)
    feature = jnp.full(shape, -1, jnp.int32)
    for s in range(16):
        rel = ((s & 7) << 1) | (s >> 3)
        here = (at >= SLOT * s) & (at < SLOT * s + ROWS)
        feature = jnp.where(here, (me ^ rel) * ROWS + at - SLOT * s, feature)
    return feature


def one_hot(hits):
    return jnp.where(hits, 1.0, 0.0).astype(BF16)


def key_of_token(shape, dim):
    at = iota(shape, dim)
    second = at >= FSLOT
    t = jnp.where(second, at - FSLOT, at)
    row = (t * 9363) >> 17
    col = t - row * SIDE
    key = (row >> 1) * PSIDE + (col >> 1) + jnp.where(second, 64, 0)
    return jnp.where(t < FRAME_TOK, key, -1)


def shard_kernel(qkv_hbm, out_hbm, own_ref, qkv_ref, out_ref, sems):
    loads = (
        pltpu.make_async_copy(qkv_hbm, qkv_ref, sems.at[0]),
        pltpu.make_async_copy(out_hbm, out_ref, sems.at[1]),
    )
    for load in loads:
        load.start()
    for load in loads:
        load.wait()
    y = lax.axis_index("seq")
    for s in range(2):

        @pl.when(y == s)
        def _():
            for part in range(3):
                at = part * D + s * HALF
                own_ref[:, part * HALF : (part + 1) * HALF] = qkv_ref[:, at : at + HALF]

    own_ref[:, QKV:] = out_ref[...]


def standardize(values):
    centered = values - jnp.mean(values, axis=-1, keepdims=True)
    inverse = lax.rsqrt(jnp.mean(centered * centered, axis=-1, keepdims=True) + 1e-05)
    return centered * inverse, inverse


def warm_kernel(second_ref, gain_ref, second_out, gain_out):
    second_out[...] = second_ref[...]
    gain_out[...] = gain_ref[...]


def prep_kernel(own_ref, peer_ref, gain_ref, rel_ref, relt_ref, pool_ref, poolt_ref, order_ref):
    order = one_hot(iota((D, REL), 0) == feature_of_slot((1, REL), 1))
    order_t = one_hot(feature_of_slot((REL, 1), 0) == iota((REL, D), 1))
    order_ref[...] = order
    gain = gain_ref[...].reshape(1, D)
    for f, src in enumerate((own_ref, peer_ref)):
        normed = (standardize(src[...].astype(F32))[0] * gain).astype(BF16)
        normed = jnp.concatenate([normed, jnp.zeros((FSLOT - FRAME_TOK, D), BF16)], axis=0)
        rel_ref[f * FSLOT : (f + 1) * FSLOT, :] = dot(normed, order).astype(BF16)
        relt_ref[f] = dot(order_t, normed, NT).astype(BF16)
    table = one_hot(iota((KEYS, TOK2), 0) == key_of_token((1, TOK2), 1)) * BF16(0.25)
    pooled = dot(table, rel_ref[...])
    hi = pooled.astype(BF16)
    pool_ref[:KEYS, :] = hi
    pool_ref[KEYS:, :] = (pooled - hi.astype(F32)).astype(BF16)
    pooled_t = dot(relt_ref[0], table[:, :FSLOT], NT) + dot(relt_ref[1], table[:, FSLOT:], NT)
    hi_t = pooled_t.astype(BF16)
    poolt_ref[:, :KEYS] = hi_t
    poolt_ref[:, KEYS:] = (pooled_t - hi_t.astype(F32)).astype(BF16)


def head_lanes(h):
    lane = iota((1, HALF), 1)
    return (lane >= h * HEAD) & (lane < (h + 1) * HEAD)


def pre_kernel(rel_ref, pool_ref, order_ref, *rest):
    blocks, (w_ref, q_ref, kv_ref, sel_ref) = rest[:EARLY], rest[EARLY:]
    for s in range(EARLY):
        at = s * SLOT
        if s < EARLY - 1:
            w_ref[at + 32 : at + SLOT, :] = jnp.zeros((16, SHARD), BF16)
            w_ref[at : at + ROWS, :] = blocks[s][...]
        else:
            w_ref[at:LOW, :] = blocks[s][: LOW - at, :]
    q_ref[...] = dot(rel_ref[:, :LOW], w_ref[:, :HALF])
    kv_ref[...] = dot(pool_ref[:, :LOW], w_ref[:, 256:QKV])
    first = pl.multiple_of(lax.axis_index("seq") * HALF, HALF)
    sel_ref[...] = dot(order_ref[pl.ds(first, HALF), :LOW], w_ref[:, QKV:])


def weight_grads(half, grad_scale, relt_ref, poolt_ref, dq_ref, e_ref, g_ref, out_ref):
    rows = slice(half * 8 * SLOT, (half + 1) * 8 * SLOT)
    g_q = dot(relt_ref[0, rows, :], dq_ref[:FSLOT, :]) + dot(relt_ref[1, rows, :], dq_ref[FSLOT:, :])
    g_kv = dot(poolt_ref[rows, :], e_ref[...]) * 4.0
    g_ref[:, :256] = g_q[:, :256] * grad_scale
    g_ref[:, 256:384] = (g_q[:, 256:] + g_kv[:, :128]) * grad_scale
    g_ref[:, 384:] = g_kv[:, 128:] * grad_scale
    for s in range(8):
        out_ref[s] = g_ref[s * SLOT : s * SLOT + ROWS, :].astype(BF16)


def own_kernel(grad_scale, relt_ref, poolt_ref, dq_ref, e_ref, out_ref, g_ref):
    weight_grads(0, grad_scale, relt_ref, poolt_ref, dq_ref, e_ref, g_ref, out_ref)


def main_kernel(grad_scale, valid_ref, rel_ref, relt_ref, pool_ref, poolt_ref, order_ref, down_ref, dpeer_ref, *rest):
    q_ref, kv_ref, sel_ref = rest[:3]
    blocks, rest = rest[3 : 20 - EARLY], rest[20 - EARLY :]
    goth_ref, w_ref, dq_ref, e_ref, mixed_ref, outh_ref = rest[:6]
    cot_ref, kbig_ref, vbig_ref, s_ref, p_ref, ds_ref, g_ref = rest[6:]
    y = lax.axis_index("seq")
    scale = 1.0 / math.sqrt(HEAD)
    straddle = LOW - (EARLY - 1) * SLOT
    w_ref[:16, :] = jnp.zeros((16, SHARD), BF16)
    w_ref[: ROWS - straddle, :] = blocks[0][straddle:, :]
    for s in range(EARLY, 16):
        at = s * SLOT - LOW
        w_ref[at + 32 : at + SLOT, :] = jnp.zeros((16, SHARD), BF16)
        w_ref[at : at + ROWS, :] = blocks[s - EARLY + 1][...]
    for f, src in enumerate((down_ref, dpeer_ref)):
        at = f * FSLOT
        cot_ref[at + 192 : at + FSLOT, :] = jnp.zeros((16, D), BF16)
        cot_ref[at : at + FRAME_TOK, :] = src[...]

    queries = (q_ref[...] + dot(rel_ref[:, LOW:], w_ref[:, :HALF])).astype(BF16)
    kv = kv_ref[...] + dot(pool_ref[:, LOW:], w_ref[:, 256:QKV])
    kv = kv[:KEYS] + kv[KEYS:]
    keys = kv[:, 32 : 32 + HALF].astype(BF16)
    values = kv[:, 32 + HALF :].astype(BF16)
    for h in range(HERE):
        lanes = head_lanes(h)
        kbig_ref[h * KEYS : (h + 1) * KEYS, :] = jnp.where(lanes, keys, BF16(0))
        vbig_ref[h * KEYS : (h + 1) * KEYS, :] = jnp.where(lanes, values, BF16(0))
    select = order_ref[pl.ds(pl.multiple_of(y * HALF, HALF), HALF), LOW:]
    outh_ref[...] = (sel_ref[...] + dot(select, w_ref[:, QKV:])).astype(BF16)
    d_mixed = dot(cot_ref[...], outh_ref[...], NT).astype(BF16)

    s_ref[...] = dot(queries, kbig_ref[...], NT)
    key = iota((1, KEYS), 1)
    late = key >= 64
    frame = jnp.where(late, 1 - y, y)
    live = (jnp.where(late, key - 64, key) < PFRAME) & (frame < valid_ref[0])
    for h in range(HERE):
        cols = slice(h * KEYS, (h + 1) * KEYS)
        for f in range(2):
            rows = slice(f * FSLOT, (f + 1) * FSLOT)
            masked = jnp.where(live, s_ref[rows, cols] * scale, -jnp.inf)
            raised = jnp.exp(masked - jnp.max(masked, axis=-1, keepdims=True))
            p_ref[rows, cols] = (raised / jnp.sum(raised, axis=-1, keepdims=True)).astype(BF16)
    mixed_ref[...] = dot(p_ref[...], vbig_ref[...]).astype(BF16)
    s_ref[...] = dot(d_mixed, vbig_ref[...], NT)
    for h in range(HERE):
        cols = slice(h * KEYS, (h + 1) * KEYS)
        for f in range(2):
            rows = slice(f * FSLOT, (f + 1) * FSLOT)
            wide = p_ref[rows, cols].astype(F32)
            d_probs = s_ref[rows, cols]
            delta = jnp.sum(wide * d_probs, axis=-1, keepdims=True)
            ds_ref[rows, cols] = (wide * (d_probs - delta) * scale).astype(BF16)
    dq_ref[:, 256:384] = jnp.zeros((TOK2, 128), BF16)
    dq_ref[:, :HALF] = dot(ds_ref[...], kbig_ref[...]).astype(BF16)

    def by_head(big):
        return sum(jnp.where(head_lanes(h), big[h * KEYS : (h + 1) * KEYS], 0.0) for h in range(HERE))

    d_keys = by_head(dot(ds_ref[...], queries, TN)) * 0.25
    d_values = by_head(dot(p_ref[...], d_mixed, TN)) * 0.25
    e = jnp.concatenate([jnp.zeros((KEYS, 32), F32), d_keys, d_values], axis=1).astype(BF16)
    e_ref[:KEYS, :] = e
    e_ref[KEYS:, :] = e
    weight_grads(1, grad_scale, relt_ref, poolt_ref, dq_ref, e_ref, g_ref, goth_ref)


def d_normed_of(f, low_ref, high_ref, dq_ref, e_ref):
    rows = slice(f * FSLOT, (f + 1) * FSLOT)
    keys = key_of_token((TOK2, 1), 0)[rows]
    d_tokens = dot(one_hot(keys == iota((FSLOT, KEYS), 1)), e_ref[:KEYS, :]).astype(BF16)
    d_queries = dq_ref[rows, :]
    return jnp.concatenate(
        [dot(d_queries, w[:, :384], NT) + dot(d_tokens, w[:, 256:QKV], NT) for w in (low_ref, high_ref)], axis=1
    )


def cross_kernel(low_ref, high_ref, dq_ref, e_ref, mixed_ref, order_ref, send_ref):
    peer = dot(d_normed_of(1, low_ref, high_ref, dq_ref, e_ref).astype(BF16), order_ref[...], NT)
    send_ref[:, :D] = peer[:FRAME_TOK].astype(BF16)
    send_ref[:, D:] = mixed_ref[FSLOT : FSLOT + FRAME_TOK, :]


def late_kernel(low_ref, high_ref, dq_ref, e_ref, own_ref):
    own_ref[...] = d_normed_of(0, low_ref, high_ref, dq_ref, e_ref).astype(BF16)


def last_kernel(
    yone_ref, second_ref, dtwo_ref, gain_ref, got_ref, own_ref, mixed_ref, outh_ref, low_ref, high_ref, order_ref, x_ref, dx_ref
):
    other = 1 - lax.axis_index("seq")
    select = order_ref[pl.ds(pl.multiple_of(other * HALF, HALF), HALF), :]
    out_other = (dot(select[:, :LOW], low_ref[:, QKV:]) + dot(select[:, LOW:], high_ref[:, QKV:])).astype(BF16)
    own = dot(own_ref[...], order_ref[...], NT)[:FRAME_TOK]
    branch = dot(mixed_ref[:FRAME_TOK, :], outh_ref[...]) + dot(got_ref[:, D:], out_other)
    x_ref[...] = (yone_ref[...].astype(F32) - branch).astype(BF16)
    xhat, inverse = standardize(second_ref[...].astype(F32))
    gained = (own + got_ref[:, :D].astype(F32)) * gain_ref[...].reshape(1, D)
    lower = inverse * (
        gained
        - jnp.mean(gained, axis=-1, keepdims=True)
        - xhat * jnp.mean(gained * xhat, axis=-1, keepdims=True)
    )
    dx_ref[...] = (dtwo_ref[...].astype(F32) + lower).astype(BF16)


def split_kernel(own_ref, got_ref, kept_ref, xab_ref, xb_ref, near_ref):
    for ref, s in (
        (xab_ref, 7),
        (xb_ref, 5),
        (near_ref.at[0], 3),
        (near_ref.at[1], 1),
        (kept_ref.at[3], 6),
        (kept_ref.at[2], 4),
        (kept_ref.at[1], 2),
        (kept_ref.at[0], 0),
    ):
        ref[...] = (own_ref[s].astype(F32) + got_ref[s].astype(F32)).astype(BF16)


def store_parts(total, cross_ref, stay_ref):
    y = lax.axis_index("seq")

    @pl.when(y == 0)
    def _():
        cross_ref[...] = total[:, 2 * HALF :].astype(cross_ref.dtype)
        stay_ref[...] = total[:, : 2 * HALF].astype(stay_ref.dtype)

    @pl.when(y == 1)
    def _():
        cross_ref[...] = total[:, :HALF].astype(cross_ref.dtype)
        stay_ref[...] = total[:, HALF:].astype(stay_ref.dtype)


def add_kernel(at, kept_ref, got_ref, sum_ref):
    sum_ref[...] = (kept_ref[at].astype(F32) + got_ref[...].astype(F32)).astype(BF16)


def part_kernel(at, kept_ref, got_ref, cross_ref, stay_ref):
    store_parts(kept_ref[at].astype(F32) + got_ref[...].astype(F32), cross_ref, stay_ref)


def near_kernel(kept_ref, got_ref, a_ref, o_ref):
    a_ref[...] = (kept_ref[1].astype(F32) + got_ref[0].astype(F32)).astype(BF16)
    o_ref[...] = kept_ref[0].astype(F32) + got_ref[1].astype(F32)


def sum_kernel(o_ref, a_ref, ab_ref, b_ref, cross_ref, stay_ref):
    total = o_ref[...] + a_ref[...].astype(F32) + ab_ref[...].astype(F32)
    y = lax.axis_index("seq")

    @pl.when(y == 0)
    def _():
        cross_ref[...] = (total[:, 2 * HALF :] + b_ref[...].astype(F32)).astype(BF16)
        stay_ref[...] = total[:, : 2 * HALF]

    @pl.when(y == 1)
    def _():
        cross_ref[...] = (total[:, :HALF] + b_ref[...].astype(F32)).astype(BF16)
        stay_ref[...] = total[:, HALF:]


def join_kernel(crossed_ref, *refs):
    grad_ref = refs[-1]
    total = sum(term[...].astype(F32) for term in refs[:-1])
    grad_ref[:, :HALF] = total[:, :HALF]
    grad_ref[:, HALF : 2 * HALF] = crossed_ref[...].astype(F32)
    grad_ref[:, 2 * HALF :] = total[:, HALF:]


def shape(*dims, kind=BF16):
    return jax.ShapeDtypeStruct(dims, kind)


def call(kernel, outs, args, scratch=(), smem=0, hbm=False, flops=0, moved=0, limit=16 << 10):
    vmem = pl.BlockSpec(memory_space=pltpu.VMEM)
    source = pl.BlockSpec(memory_space=pltpu.HBM) if hbm else vmem
    return pl.pallas_call(
        kernel,
        out_shape=outs,
        in_specs=[pl.BlockSpec(memory_space=pltpu.SMEM)] * smem + [source] * (len(args) - smem),
        out_specs=jax.tree.map(lambda _: vmem, outs),
        scratch_shapes=scratch,
        compiler_params=pltpu.CompilerParams(vmem_limit_bytes=limit << 10),
        cost_estimate=pl.CostEstimate(flops=flops, bytes_accessed=moved, transcendentals=0),
    )(*args)


def paired_body(y_one, second_stream, d_one, d_two, layer_norm_gain, w_qkv, w_out, frames_valid):
    grad_scale = 1.0 / math.sqrt(lax.axis_size("dp") * 2 * FRAME_TOK)
    second, cot = second_stream[0], d_one[0]
    gain = layer_norm_gain

    own = call(
        shard_kernel,
        shape(ROWS, SHARD),
        (w_qkv, w_out),
        scratch=(
            pltpu.VMEM((ROWS, 2 * QKV), BF16),
            pltpu.VMEM((ROWS, D), BF16),
            pltpu.SemaphoreType.DMA((2,)),
        ),
        hbm=True,
        moved=400_000,
        limit=60 << 10,
    )
    by_b = swap(own, OVER_Z2)
    by_x = swap(own, OVER_X)
    by_a = swap(own, OVER_Z1)
    second_peer = swap(second, OVER_Y)
    cot_peer = swap(cot, OVER_Y)
    by_ab = swap(by_b, OVER_Z1)
    by_xb = swap(by_b, OVER_X)
    by_xa = swap(by_a, OVER_X)
    by_xab = swap(by_ab, OVER_X)
    mine = (own, by_x, by_a, by_xa, by_b, by_xb, by_ab, by_xab)
    other = tuple(swap(block, OVER_CORE) for block in mine)

    second_here, gain_here = call(
        warm_kernel, (shape(FRAME_TOK, D), shape(D, kind=F32)), (second, gain), moved=500_000
    )
    rel, rel_t, pool, pool_t, order = call(
        prep_kernel,
        (shape(TOK2, REL), shape(2, REL, FSLOT), shape(2 * KEYS, REL), shape(REL, 2 * KEYS), shape(D, REL)),
        (second_here, second_peer, gain_here),
        flops=1_200_000_000,
        moved=3_000_000,
    )
    blocks = mine + other
    w_low, q_low, kv_low, sel_low = call(
        pre_kernel,
        (
            shape(LOW, SHARD),
            shape(TOK2, HALF, kind=F32),
            shape(2 * KEYS, 608, kind=F32),
            shape(HALF, D, kind=F32),
        ),
        (rel, pool, order) + blocks[:EARLY],
        flops=800_000_000,
        moved=4_000_000,
    )
    g_oth, w_high, d_q, e, mixed, out_own = call(
        functools.partial(main_kernel, grad_scale),
        (
            shape(8, ROWS, QKV),
            shape(REL - LOW, SHARD),
            shape(TOK2, 384),
            shape(2 * KEYS, 608),
            shape(TOK2, HALF),
            shape(HALF, D),
        ),
        (frames_valid, rel, rel_t, pool, pool_t, order, cot, cot_peer, q_low, kv_low, sel_low) + blocks[EARLY - 1 :],
        scratch=(
            pltpu.VMEM((TOK2, D), BF16),
            pltpu.VMEM((KLANES, HALF), BF16),
            pltpu.VMEM((KLANES, HALF), BF16),
            pltpu.VMEM((TOK2, KLANES), F32),
            pltpu.VMEM((TOK2, KLANES), BF16),
            pltpu.VMEM((TOK2, KLANES), BF16),
            pltpu.VMEM((8 * SLOT, QKV), F32),
        ),
        smem=1,
        flops=4_000_000_000,
        moved=8_000_000,
        limit=32 << 10,
    )

    g_own = call(
        functools.partial(own_kernel, grad_scale),
        shape(8, ROWS, QKV),
        (rel_t, pool_t, d_q, e),
        scratch=(pltpu.VMEM((8 * SLOT, QKV), F32),),
        flops=500_000_000,
        moved=2_000_000,
    )
    block, pair = shape(ROWS, QKV), shape(2, ROWS, QKV)
    wide = shape(ROWS, QKV, kind=F32)
    kept, x_ab, x_b, near = call(
        split_kernel,
        (shape(4, ROWS, QKV), block, block, pair),
        (g_own, swap(g_oth, OVER_CORE)),
        moved=1_500_000,
    )
    got_ab, got_b = swap(x_ab, OVER_X), swap(x_b, OVER_X)
    to_ab = call(functools.partial(add_kernel, 3), block, (kept, got_ab), moved=200_000)
    to_b = call(
        functools.partial(part_kernel, 2),
        (shape(ROWS, HALF), shape(ROWS, 2 * HALF)),
        (kept, got_b),
        moved=200_000,
    )
    to_a, here = call(near_kernel, (block, wide), (kept, swap(near, OVER_X)), moved=400_000)
    from_ab = swap(to_ab, OVER_Z1 | OVER_Z2)
    from_b, from_b_stay = swap(to_b[0], OVER_Z2), swap(to_b[1], OVER_Z2)
    from_a = swap(to_a, OVER_Z1)
    crossing, stay = call(
        sum_kernel,
        (shape(ROWS, HALF), shape(ROWS, 2 * HALF, kind=F32)),
        (here, from_a, from_ab, from_b),
        moved=400_000,
    )
    crossed = swap(crossing, OVER_Y)
    grad_qkv = call(join_kernel, wide, (crossed, stay, from_b_stay), moved=300_000)

    send = call(
        cross_kernel,
        shape(FRAME_TOK, SEND),
        (w_low, w_high, d_q, e, mixed, order),
        flops=600_000_000,
        moved=4_000_000,
    )
    got = swap(send, OVER_Y)
    d_normed = call(
        late_kernel,
        shape(FSLOT, REL),
        (w_low, w_high, d_q, e),
        flops=1_000_000_000,
        moved=3_000_000,
    )
    x_one, dx_two = call(
        last_kernel,
        (shape(FRAME_TOK, D), shape(FRAME_TOK, D)),
        (y_one[0], second_here, d_two[0], gain_here, got, d_normed, mixed, out_own, w_low, w_high, order),
        flops=300_000_000,
        moved=3_000_000,
    )
    return (x_one[None], dx_two[None], grad_qkv)


def local_paired(*args):
    return paired_body(*args)


def solution(mesh):
    in_specs = (
        P("dp", "seq", None),
        P("dp", "seq", None),
        P("dp", "seq", None),
        P("dp", "seq", None),
        P(),
        P("dp", None),
        P("dp", None),
        P("dp"),
    )
    out_specs = (P("dp", "seq", None), P("dp", "seq", None), P("dp", "seq"))
    paired = dict(mesh.shape) == {"dp": 16, "seq": 2}
    local = local_paired if paired else local_general
    return jax.shard_map(local, mesh=mesh, in_specs=in_specs, out_specs=out_specs, check_vma=False)
```
